768 devices in a mesh: lat: 48 (over x, z), lev: 16 (over y, core).
Axes of the slice: x: 4, y: 8, z: 12, core: 2. Of those that a mesh axis runs over, the one named last changes fastest.
Arguments:
- grid_field: bfloat16 [32, 30720, 128], P('lev', 'lat'), may hold values from -6 to 6
- send_blocks: int32 [48, 2, 128], P('lat'), may hold values from 0 to 639
- donor_index: int32 [30720, 2], P('lat'), may hold values from 0 to 895
- tile_choice: int32 [30720, 2], P('lat'), may hold values from 0 to 7
- kernel_tiles: bfloat16 [8, 128, 128], replicated, may hold values from -0.375 to 0.375
- circle_len: int32 [768], replicated, may hold values from 20 to 5120, as said below
- slot_wave: int32 [1536], replicated, may hold values from 0 to 1535, each once
- legendre: bfloat16 [1536, 768, 1280], P(('lat', 'lev')), may hold values from -0.0024414062 to 0.0024414062
Outputs:
- spectra: bfloat16 [32, 2, 1536, 1280], P(None, None, ('lat', 'lev'))
The draws below stay inside these ranges and needn't reach their ends.
Inputs may be any that keep to these rules, and one draw needn't show every extreme that they name: `circle_len`: each circle has 4 i + 16 points for a whole i of 1 or more, and some circle has 5120.
All inputs are finite; a program needn't handle non-finite values.
Results may differ from the reference program's by a relative error of at most 0.007.
Values may be sent and summed in bfloat16 or wider, within the bound.
A program may use at most 64 MiB of HBM per device.

```python
import math
import jax
import jax.numpy as jnp
from jax import lax

PTS = 5120
NW = 1280
KT = 8
BANDS = 48
LEVELS = 32
CIRCLES_PER_BAND = 16
CAP = 128
CIRCLES = 768
BAND_BLOCKS = 640
MSLOTS = 1536


def draw_circle_len(key, part):
    base_key = jax.random.fold_in(key, 17)
    key_step, key_widest = jax.random.split(base_key)
    top_step = (PTS - 16) // 4
    latitude_step = jax.random.randint(key_step, (CIRCLES,), 1, top_step + 1)
    widest = jax.random.randint(key_widest, (), 0, CIRCLES)
    lengths = 4 * latitude_step + 16
    return jnp.where(jnp.arange(CIRCLES) == widest, 4 * top_step + 16, lengths).astype(jnp.int32)


def touch_ends(values, rng, low, high):
    spot = [jax.random.randint(jax.random.fold_in(rng, axis), (), 0, length) for axis, length in enumerate(values.shape)]
    widest = values.shape.index(max(values.shape))
    beside = spot[:widest] + [(spot[widest] + 1) % values.shape[widest]] + spot[widest + 1:]
    return values.at[tuple(spot)].set(low).at[tuple(beside)].set(high)


def block_scale(rng, shape, cuts, least, high):
    factor_of, own = 1.0, jax.random.fold_in(rng, 6)
    for dim, blocks in cuts:
        steps = jnp.exp(jax.random.uniform(jax.random.fold_in(own, dim), (blocks,), jnp.float32, least / len(cuts), high / len(cuts)))
        factor_of = factor_of * jnp.repeat(steps, shape[dim] // blocks).reshape([-1 if axis == dim else 1 for axis in range(len(shape))])
    return factor_of


def scatter_about(stream_key, shape, deviation, limit, cuts=(), kind=jnp.bfloat16):
    gain = block_scale(stream_key, shape, cuts, -0.22, 0.18) if cuts else 1.0
    array = jax.random.normal(stream_key, shape, jnp.float32) * deviation * gain
    return jnp.minimum(jnp.maximum(array, -limit), limit).astype(kind)


def setup_inputs(seed: int = 0) -> dict:
    key_of = jax.random.split(jax.random.key(seed), 9)
    return {
        "grid_field": scatter_about(key_of[0], (LEVELS, CIRCLES * PTS // 128, 128), 1.0, 6.0, ((0, 16), (1, 48))),
        "send_blocks": touch_ends(jax.random.randint(key_of[1], (BANDS, 2, CAP), 0, BAND_BLOCKS), jax.random.fold_in(key_of[1], 1), 0, BAND_BLOCKS - 1).astype(jnp.int32),
        "donor_index": touch_ends(jax.random.randint(key_of[2], (CIRCLES * PTS // 128, 2), 0, BAND_BLOCKS + 2 * CAP), jax.random.fold_in(key_of[2], 1), 0, (BAND_BLOCKS + 2 * CAP) - 1).astype(jnp.int32),
        "tile_choice": touch_ends(jax.random.randint(key_of[3], (CIRCLES * PTS // 128, 2), 0, KT), jax.random.fold_in(key_of[3], 1), 0, KT - 1).astype(jnp.int32),
        "kernel_tiles": scatter_about(key_of[4], (KT, 128, 128), 256 ** -0.5, 0.375),
        "circle_len": draw_circle_len(jax.random.fold_in(key_of[8], 71), 0),
        "slot_wave": jax.random.permutation(key_of[6], MSLOTS).astype(jnp.int32),
        "legendre": scatter_about(key_of[7], (MSLOTS, CIRCLES, NW), (3 * CIRCLES * PTS // 2) ** -0.5, 0.0024414062, ((0, 768),)),
    }


def circle_table(length, waves, points, top_wave):
    live_slot = (waves >= 1) & (waves < top_wave) & (2 * waves < length)
    step_angle = (2.0 * math.pi) / length.astype(jnp.float32)
    phases = (jnp.arange(points, dtype=jnp.int32)[:, None] * waves[None, :]) % length
    angles = phases.astype(jnp.float32) * step_angle
    keep_mask = (jnp.arange(points, dtype=jnp.int32) < length)[:, None] & live_slot[None, :]
    cosine = jnp.where(keep_mask, jnp.cos(angles), 0.0)
    sine_part = jnp.where(keep_mask, -jnp.sin(angles), 0.0)
    return jnp.concatenate([cosine, sine_part], axis=1).astype(jnp.bfloat16)


def reference(grid_field, send_blocks, donor_index, tile_choice, kernel_tiles, circle_len, slot_wave, legendre):
    bands = grid_field.reshape(LEVELS, BANDS, BAND_BLOCKS, 128)
    donor_band = donor_index.reshape(BANDS, BAND_BLOCKS, 2)
    tile_band = tile_choice.reshape(BANDS, BAND_BLOCKS, 2)
    kernels = kernel_tiles.astype(jnp.float32)

    def one_band(band):
        own = lax.dynamic_index_in_dim(bands, band, 1, keepdims=False)
        below = jnp.maximum(band - 1, 0).astype(jnp.int32)
        above = jnp.minimum(band + 1, BANDS - 1).astype(jnp.int32)
        from_below = jnp.take(lax.dynamic_index_in_dim(bands, below, 1, keepdims=False), send_blocks[below, 1], axis=1)
        from_above = jnp.take(lax.dynamic_index_in_dim(bands, above, 1, keepdims=False), send_blocks[above, 0], axis=1)
        from_below = jnp.where(band > 0, from_below, jnp.zeros_like(from_below))
        from_above = jnp.where(band < BANDS - 1, from_above, jnp.zeros_like(from_above))
        donor_pool = jnp.concatenate([own, from_below, from_above], axis=1)
        picked = jnp.take(donor_pool, donor_band[band].reshape(-1), axis=1)
        picked = picked.reshape(LEVELS, BAND_BLOCKS, 2, 128).astype(jnp.float32)
        weights = kernels[tile_band[band]]
        arrival = jnp.einsum("lbkc,bkcd->lbd", picked, weights, precision=lax.Precision.HIGHEST)
        return (arrival * arrival).astype(jnp.bfloat16)

    squared = lax.map(one_band, jnp.arange(BANDS, dtype=jnp.int32))
    squared = squared.reshape(BANDS, LEVELS, CIRCLES_PER_BAND, PTS).transpose(1, 0, 2, 3).reshape(LEVELS, CIRCLES, PTS)

    def one_circle(operands):
        values, length = operands
        factors = circle_table(length, slot_wave, PTS, NW).astype(jnp.float32)
        grand_total = jnp.dot(values.astype(jnp.float32), factors, precision=lax.Precision.HIGHEST, preferred_element_type=jnp.float32)
        return grand_total.astype(jnp.bfloat16)

    coeffs = lax.map(one_circle, (jnp.moveaxis(squared, 1, 0), circle_len))
    coeffs = coeffs.reshape(CIRCLES, LEVELS, 2, MSLOTS).transpose(3, 0, 1, 2)
    wave_all = jnp.arange(NW, dtype=jnp.int32)

    def one_slot(operands):
        block_piece, lookup_table_rows, wave = operands
        grand_total = jnp.einsum("ump,uv->mpv", block_piece.astype(jnp.float32), lookup_table_rows.astype(jnp.float32), precision=lax.Precision.HIGHEST)
        return jnp.where(wave_all[None, None, :] >= wave, grand_total, 0.0).astype(jnp.bfloat16)

    spectra = lax.map(one_slot, (coeffs, legendre, slot_wave))
    return spectra.transpose(1, 2, 0, 3)
```

```python
import functools

import jax
import jax.numpy as jnp
from jax import lax
from jax.experimental import pallas as pl
from jax.experimental.pallas import tpu as pltpu
from jax.sharding import PartitionSpec as P

PTS = 5120
FINE = 128
CHUNK = 256

SIN_COEF = (3.1415927410125732, -5.167709827423096, 2.550076961517334, -0.5982874631881714, 0.07764891535043716)
COS_COEF = (1.0, -4.934792518615723, 4.058409690856934, -1.331863284111023, 0.21965928375720978)


def poly(coef, x):
    acc = jnp.full_like(x, coef[-1])
    for c in coef[-2::-1]:
        acc = acc * x + c
    return acc


def phase(steps, length, inverse):
    turns = jnp.floor(steps * inverse + 0.5)
    u = (steps - turns * length) * inverse
    u2 = u * u
    s = u * poly(SIN_COEF, u2)
    c = poly(COS_COEF, u2)
    return 1.0 - 2.0 * s * s, -2.0 * s * c


def times(a, b):
    return a[0] * b[0] - a[1] * b[1], a[0] * b[1] + a[1] * b[0]


def local_kernel(
    top_wave, grid_ref, below_ref, above_ref, donor_ref, tile_ref, kern_ref, len_ref, wave_ref,
    out_ref, pool_scr, diag_scr, idx_scr, x_scr, len_scr, coef_scr
):
    levels, blocks, lanes = grid_ref.shape
    cap = below_ref.shape[1]
    pool_size = blocks + 2 * cap
    tiles = kern_ref.shape[0]
    circles = x_scr.shape[0]
    per_circle = blocks // circles
    width = levels * lanes
    band = lax.axis_index("lat")

    for l in range(levels):
        cols = slice(l * lanes, (l + 1) * lanes)
        pool_scr[0:blocks, cols] = grid_ref[l]
        pool_scr[blocks : blocks + cap, cols] = below_ref[l]
        pool_scr[blocks + cap : pool_size, cols] = above_ref[l]
    diag_scr[...] = jnp.zeros_like(diag_scr)
    for t in range(tiles):
        for l in range(levels):
            cols = slice(l * lanes, (l + 1) * lanes)
            diag_scr[t, cols, cols] = kern_ref[t]
    idx_scr[...] = jnp.zeros_like(idx_scr)
    idx_scr[0:2, :] = donor_ref[...].astype(jnp.float32)
    idx_scr[2:4, :] = tile_ref[...].astype(jnp.float32)
    columns = idx_scr[...].T

    group = 4
    rows = group * per_circle
    for start in range(0, circles, group):
        part = columns[start * per_circle : (start + group) * per_circle, :]
        total = jnp.zeros((rows, width), jnp.float32)
        spots = lax.broadcasted_iota(jnp.int32, (rows, pool_size), 1).astype(jnp.float32)
        for k in range(2):
            hot = jnp.where(spots == part[:, k : k + 1], 1.0, 0.0).astype(jnp.bfloat16)
            picked = jnp.dot(hot, pool_scr[...], preferred_element_type=jnp.float32)
            which = part[:, 2 + k : 3 + k]
            for t in range(tiles):
                chosen = jnp.where(which == float(t), picked, 0.0).astype(jnp.bfloat16)
                total += jnp.dot(chosen, diag_scr[t], preferred_element_type=jnp.float32)
        squared = total * total
        for c in range(group):
            n = len_ref[band * circles + start + c]
            spot = lax.broadcasted_iota(jnp.int32, (per_circle, lanes), 0) * lanes
            spot = spot + lax.broadcasted_iota(jnp.int32, (per_circle, lanes), 1)
            for l in range(levels):
                piece = squared[c * per_circle : (c + 1) * per_circle, l * lanes : (l + 1) * lanes]
                piece = jnp.where(spot < n, piece, 0.0).astype(jnp.bfloat16)
                x_scr[start + c, 48 * l : 48 * l + per_circle, :] = piece
            len_scr[start + c : start + c + 1, :] = jnp.full((1, CHUNK), n, jnp.int32).astype(jnp.float32)

    slots = wave_ref.shape[1]
    row = lax.broadcasted_iota(jnp.int32, (8, CHUNK), 0).astype(jnp.float32)
    for chunk in range(slots // CHUNK):
        span = slice(chunk * CHUNK, (chunk + 1) * CHUNK)
        wave = wave_ref[:, span]
        wave_rows = row * wave

        def circle(g, carry):
            length = len_scr[pl.ds(g, 1), :]
            inverse = 1.0 / length
            base = phase(wave_rows, length, inverse)
            outer = phase(wave_rows * float(FINE), length, inverse)
            step = times((base[0][7:8], base[1][7:8]), (base[0][1:2], base[1][1:2]))
            jump = times((outer[0][7:8], outer[1][7:8]), (outer[0][1:2], outer[1][1:2]))
            twice = jnp.broadcast_to(2.0 * step[0], base[0].shape)
            second = times(base, step)
            cos_rows, sin_rows = [base[0], second[0]], [base[1], second[1]]
            for q in range(2, FINE // 8):
                cos_rows.append(twice * cos_rows[-1] - cos_rows[-2])
                sin_rows.append(twice * sin_rows[-1] - sin_rows[-2])
            cos_table = jnp.concatenate(cos_rows, axis=0).astype(jnp.bfloat16)
            sin_table = jnp.concatenate(sin_rows, axis=0).astype(jnp.bfloat16)
            x = x_scr[g]
            real = jnp.dot(x, cos_table, preferred_element_type=jnp.float32)
            imag = jnp.dot(x, sin_table, preferred_element_type=jnp.float32)
            jump = (jnp.broadcast_to(jump[0], row.shape), jnp.broadcast_to(jump[1], row.shape))
            live = (wave >= 1.0) & (wave < float(top_wave)) & (2.0 * wave < length)
            for l in range(levels):
                last = per_circle // 8 - 1
                at = 48 * l + 8 * last
                total = (real[at : at + 8], imag[at : at + 8])
                for q in range(last - 1, -1, -1):
                    at = 48 * l + 8 * q
                    turned = times(total, jump)
                    total = (turned[0] + real[at : at + 8], turned[1] + imag[at : at + 8])
                total = times(total, outer)
                for c in range(2):
                    value = jnp.sum(total[c], axis=0, keepdims=True)
                    coef_scr[2 * l + c, pl.ds(g, 1), span] = jnp.where(live, value, 0.0)
            return carry

        lax.fori_loop(0, circles, circle, 0)

    quarter = lax.broadcasted_iota(jnp.int32, (circles, 128), 1) // 32
    for block in range(slots // 128):
        parts = [coef_scr[k, :, block * 128 : (block + 1) * 128] for k in range(4)]
        for to in range(4):
            value = parts[to]
            for k in range(4):
                if k != to:
                    value = jnp.where(quarter == k, pltpu.roll(parts[k], (32 * (k - to)) % 128, 1), value)
            out_ref[block * 4 + to] = value.astype(jnp.bfloat16)


def transform_band(grid, below, above, donor, choice, kernels, lengths, waves, bands, top_wave):
    levels, blocks, lanes = grid.shape
    circles = blocks * lanes // PTS
    slots = waves.shape[1]
    vmem = pl.BlockSpec(memory_space=pltpu.VMEM)
    return pl.pallas_call(
        functools.partial(local_kernel, top_wave),
        out_shape=jax.ShapeDtypeStruct((bands, circles, 128), jnp.bfloat16),
        in_specs=[vmem] * 6 + [pl.BlockSpec(memory_space=pltpu.SMEM), vmem],
        out_specs=vmem,
        scratch_shapes=[
            pltpu.VMEM((blocks + 2 * below.shape[1], levels * lanes), jnp.bfloat16),
            pltpu.VMEM((kernels.shape[0], levels * lanes, levels * lanes), jnp.bfloat16),
            pltpu.VMEM((8, blocks), jnp.float32),
            pltpu.VMEM((circles, 96, lanes), jnp.bfloat16),
            pltpu.VMEM((circles, CHUNK), jnp.float32),
            pltpu.VMEM((4, circles, slots), jnp.float32),
        ],
        compiler_params=pltpu.CompilerParams(vmem_limit_bytes=48 * 1024 * 1024),
        name="interpolate_and_transform",
    )(grid, below, above, donor, choice, kernels, lengths, waves)


def shift_bands(outgoing, cap):
    size = lax.axis_size("lat")
    up = [(i, i + 1) for i in range(size - 1)]
    down = [(j, i) for i, j in up]
    below = lax.ppermute(outgoing[:, cap:], "lat", up)
    above = lax.ppermute(outgoing[:, :cap], "lat", down)
    return below, above


def body(
    grid_field, send_blocks, donor_index, tile_choice, kernel_tiles, circle_len, slot_wave, legendre
):
    levels, blocks, lanes = grid_field.shape
    cap = send_blocks.shape[2]
    top_wave = legendre.shape[2]
    slot_dev = legendre.shape[0]
    circles = blocks * lanes // PTS
    bands = lax.axis_size("lat")
    level_groups = lax.axis_size("lev")
    slots = slot_wave.shape[0]
    outgoing = jnp.take(grid_field, send_blocks[0].reshape(-1), axis=1)
    below, above = shift_bands(outgoing, cap)
    tiles_out = transform_band(
        grid_field, below, above, donor_index.T, tile_choice.T, kernel_tiles, circle_len,
        slot_wave.astype(jnp.float32).reshape(1, slots), bands, top_wave,
    )
    arrived = lax.all_to_all(tiles_out, "lat", split_axis=0, concat_axis=0, tiled=True)
    arrived = arrived.reshape(bands * circles, 4, level_groups, slot_dev)
    turned = arrived.transpose(2, 1, 3, 0).reshape(level_groups, 4 * slot_dev, bands * circles)
    gathered = lax.all_to_all(turned, "lev", split_axis=0, concat_axis=0, tiled=True)
    gathered = gathered.reshape(level_groups * 4, slot_dev, bands * circles)
    spectra = jnp.einsum("rsg,sgn->rsn", gathered, legendre, preferred_element_type=jnp.float32)
    first = (lax.axis_index("lat") * level_groups + lax.axis_index("lev")) * slot_dev
    mine = lax.dynamic_slice_in_dim(slot_wave, first, slot_dev)
    allowed = jnp.arange(top_wave, dtype=jnp.int32)[None, :] >= mine[:, None]
    spectra = jnp.where(allowed[None], spectra, 0.0).astype(jnp.bfloat16)
    return spectra.reshape(level_groups * levels, 2, slot_dev, top_wave)


def solution(mesh):
    return jax.shard_map(
        body,
        mesh=mesh,
        in_specs=(
            P("lev", "lat", None),
            P("lat", None, None),
            P("lat", None),
            P("lat", None),
            P(),
            P(),
            P(),
            P(("lat", "lev"), None, None),
        ),
        out_specs=P(None, None, ("lat", "lev"), None),
        check_vma=False,
    )
```

```python
import functools

import jax
import jax.numpy as jnp
from jax import lax
from jax.experimental import pallas as pl
from jax.experimental.pallas import tpu as pltpu
from jax.sharding import PartitionSpec as P

PTS = 5120
FINE = 128
CHUNK = 256
PAIR = 2

SIN_COEF = (3.1415927410125732, -5.167709827423096, 2.550076961517334, -0.5982874631881714, 0.07764891535043716)
COS_COEF = (1.0, -4.934792518615723, 4.058409690856934, -1.331863284111023, 0.21965928375720978)


def poly(coef, x):
    acc = jnp.full_like(x, coef[-1])
    for c in coef[-2::-1]:
        acc = acc * x + c
    return acc


def phase(steps, length, inverse):
    turns = jnp.floor(steps * inverse + 0.5)
    u = (steps - turns * length) * inverse
    u2 = u * u
    s = u * poly(SIN_COEF, u2)
    c = poly(COS_COEF, u2)
    return 1.0 - 2.0 * s * s, -2.0 * s * c


def times(a, b):
    return a[0] * b[0] - a[1] * b[1], a[0] * b[1] + a[1] * b[0]


MESH = pl.DeviceIdType.MESH


def fill_donors(grid_ref, below_ref, above_ref, donor_ref, tile_ref, kern_ref, pool_scr, diag_scr, idx_scr):
    levels, blocks, lanes = grid_ref.shape
    cap = below_ref.shape[1]
    for l in range(levels):
        cols = slice(l * lanes, (l + 1) * lanes)
        pool_scr[0:blocks, cols] = grid_ref[l]
        pool_scr[blocks : blocks + cap, cols] = below_ref[l]
        pool_scr[blocks + cap : blocks + 2 * cap, cols] = above_ref[l]
    diag_scr[...] = jnp.zeros_like(diag_scr)
    for t in range(kern_ref.shape[0]):
        for l in range(levels):
            cols = slice(l * lanes, (l + 1) * lanes)
            diag_scr[t, cols, cols] = kern_ref[t]
    idx_scr[...] = jnp.zeros_like(idx_scr)
    idx_scr[0:2, :] = donor_ref[...].astype(jnp.float32)
    idx_scr[2:4, :] = tile_ref[...].astype(jnp.float32)


def interpolate(band, len_ref, pool_scr, diag_scr, idx_scr, x_scr, len_scr):
    pool_size, width = pool_scr.shape
    tiles = diag_scr.shape[0]
    circles, _, lanes = x_scr.shape
    levels = width // lanes
    per_circle = idx_scr.shape[1] // circles
    columns = idx_scr[...].T
    group = 4
    rows = group * per_circle
    for start in range(0, circles, group):
        part = columns[start * per_circle : (start + group) * per_circle, :]
        total = jnp.zeros((rows, width), jnp.float32)
        spots = lax.broadcasted_iota(jnp.int32, (rows, pool_size), 1).astype(jnp.float32)
        for k in range(2):
            hot = jnp.where(spots == part[:, k : k + 1], 1.0, 0.0).astype(jnp.bfloat16)
            picked = jnp.dot(hot, pool_scr[...], preferred_element_type=jnp.float32)
            which = part[:, 2 + k : 3 + k]
            for t in range(tiles):
                chosen = jnp.where(which == float(t), picked, 0.0).astype(jnp.bfloat16)
                total += jnp.dot(chosen, diag_scr[t], preferred_element_type=jnp.float32)
        squared = total * total
        for c in range(group):
            n = len_ref[band * circles + start + c]
            spot = lax.broadcasted_iota(jnp.int32, (per_circle, lanes), 0) * lanes
            spot = spot + lax.broadcasted_iota(jnp.int32, (per_circle, lanes), 1)
            for l in range(levels):
                piece = squared[c * per_circle : (c + 1) * per_circle, l * lanes : (l + 1) * lanes]
                piece = jnp.where(spot < n, piece, 0.0).astype(jnp.bfloat16)
                x_scr[start + c, 48 * l : 48 * l + per_circle, :] = piece
            len_scr[start + c : start + c + 1, :] = jnp.full((1, CHUNK), n, jnp.int32).astype(jnp.float32)


def transform_circle(g, wave, top_wave, levels, per_circle, x_scr, len_scr, coef_scr):
    row = lax.broadcasted_iota(jnp.int32, (8, CHUNK), 0).astype(jnp.float32)
    wave_rows = row * wave
    length = len_scr[pl.ds(g, 1), :]
    inverse = 1.0 / length
    base = phase(wave_rows, length, inverse)
    outer = phase(wave_rows * float(FINE), length, inverse)
    step = times((base[0][7:8], base[1][7:8]), (base[0][1:2], base[1][1:2]))
    jump = times((outer[0][7:8], outer[1][7:8]), (outer[0][1:2], outer[1][1:2]))
    twice = jnp.broadcast_to(2.0 * step[0], base[0].shape)
    second = times(base, step)
    cos_rows, sin_rows = [base[0], second[0]], [base[1], second[1]]
    for q in range(2, FINE // 8):
        cos_rows.append(twice * cos_rows[-1] - cos_rows[-2])
        sin_rows.append(twice * sin_rows[-1] - sin_rows[-2])
    cos_table = jnp.concatenate(cos_rows, axis=0).astype(jnp.bfloat16)
    sin_table = jnp.concatenate(sin_rows, axis=0).astype(jnp.bfloat16)
    x = x_scr[g]
    real = jnp.dot(x, cos_table, preferred_element_type=jnp.float32)
    imag = jnp.dot(x, sin_table, preferred_element_type=jnp.float32)
    jump = (jnp.broadcast_to(jump[0], row.shape), jnp.broadcast_to(jump[1], row.shape))
    live = (wave >= 1.0) & (wave < float(top_wave)) & (2.0 * wave < length)
    for l in range(levels):
        last = per_circle // 8 - 1
        at = 48 * l + 8 * last
        total = (real[at : at + 8], imag[at : at + 8])
        for q in range(last - 1, -1, -1):
            at = 48 * l + 8 * q
            turned = times(total, jump)
            total = (turned[0] + real[at : at + 8], turned[1] + imag[at : at + 8])
        total = times(total, outer)
        for c in range(2):
            value = jnp.sum(total[c], axis=0, keepdims=True)
            coef_scr[2 * l + c, pl.ds(g, 1), :] = jnp.where(live, value, 0.0)


def pack_tiles(first, coef_scr, send_scr):
    circles = coef_scr.shape[1]
    quarter = lax.broadcasted_iota(jnp.int32, (circles, 128), 1) // 32
    for block in range(CHUNK // 128):
        parts = [coef_scr[k, :, block * 128 : (block + 1) * 128] for k in range(4)]
        for to in range(4):
            value = parts[to]
            for k in range(4):
                if k != to:
                    value = jnp.where(quarter == k, pltpu.roll(parts[k], (32 * (k - to)) % 128, 1), value)
            send_scr[first + block * 4 + to] = value.astype(jnp.bfloat16)


def whole_kernel(
    top_wave, bands, groups, slot_dev,
    grid_ref, below_ref, above_ref, donor_ref, tile_ref, kern_ref, len_ref, wave_ref, lane_wave_ref,
    legendre_ref, out_ref,
    pool_scr, diag_scr, idx_scr, x_scr, len_scr, coef_scr, send_lat, recv_lat, send_lev, recv_lev, leg_scr,
    sems, leg_sem
):
    levels, blocks, lanes = grid_ref.shape
    circles = x_scr.shape[0]
    per_circle = blocks // circles
    band, group = lax.axis_index("lat"), lax.axis_index("lev")
    fetch = pltpu.make_async_copy(legendre_ref, leg_scr, leg_sem)
    fetch.start()
    barrier = pltpu.get_barrier_semaphore()

    def greet_lat(i, carry):
        pl.semaphore_signal(barrier, inc=1, device_id={"lat": lax.rem(band + i, bands)}, device_id_type=MESH)
        return carry

    def greet_lev(i, carry):
        pl.semaphore_signal(barrier, inc=1, device_id={"lev": lax.rem(group + i, groups)}, device_id_type=MESH)
        return carry

    lax.fori_loop(1, bands, greet_lat, 0)
    lax.fori_loop(1, groups, greet_lev, 0)

    fill_donors(grid_ref, below_ref, above_ref, donor_ref, tile_ref, kern_ref, pool_scr, diag_scr, idx_scr)
    interpolate(band, len_ref, pool_scr, diag_scr, idx_scr, x_scr, len_scr)
    pl.semaphore_wait(barrier, bands + groups - 2)

    chunks = wave_ref.shape[0]
    per_chunk = bands // chunks

    def lat_copy(source, to):
        return pltpu.make_async_remote_copy(
            src_ref=send_lat.at[source], dst_ref=recv_lat.at[band], send_sem=sems.at[0], recv_sem=sems.at[1],
            device_id={"lat": to}, device_id_type=MESH,
        )

    def chunk_step(step, carry):
        chunk = lax.rem(step + band // per_chunk, chunks)
        wave = wave_ref[chunk]

        def circle(i, inner):
            for k in range(PAIR):
                transform_circle(i * PAIR + k, wave, top_wave, levels, per_circle, x_scr, len_scr, coef_scr)
            return inner

        lax.fori_loop(0, circles // PAIR, circle, 0)
        pack_tiles(chunk * per_chunk, coef_scr, send_lat)
        for i in range(per_chunk):
            to = chunk * per_chunk + i

            @pl.when(to != band)
            def _():
                lat_copy(to, to).start()

        return carry

    lax.fori_loop(0, chunks, chunk_step, 0)
    recv_lat[band] = send_lat[band]
    some = pl.ds(0, bands - 1)
    bulk = pltpu.make_async_remote_copy(
        src_ref=send_lat.at[some], dst_ref=recv_lat.at[some], send_sem=sems.at[0], recv_sem=sems.at[1],
        device_id={"lat": lax.rem(band + 1, bands)}, device_id_type=MESH,
    )
    bulk.wait()

    target = lax.broadcasted_iota(jnp.int32, (128, 128), 0)
    source = lax.broadcasted_iota(jnp.int32, (128, 128), 1)
    share = 4 * slot_dev
    wanted = (target % share) // slot_dev * (groups * slot_dev) + target // share * slot_dev + target % slot_dev
    pick = jnp.where(source == wanted, 1.0, 0.0).astype(jnp.bfloat16)
    arrived = recv_lat[...].reshape(bands * circles, 128)
    turned = lax.dot_general(pick, arrived, (((1,), (1,)), ((), ())), preferred_element_type=jnp.float32)
    for v in range(groups):
        send_lev[v] = turned[v * share : (v + 1) * share].astype(jnp.bfloat16)

    def send_group(i, carry):
        to = lax.rem(group + i, groups)
        pltpu.make_async_remote_copy(
            src_ref=send_lev.at[to], dst_ref=recv_lev.at[group], send_sem=sems.at[2], recv_sem=sems.at[3],
            device_id={"lev": to}, device_id_type=MESH,
        ).start()
        return carry

    lax.fori_loop(1, groups, send_group, 0)
    recv_lev[group] = send_lev[group]
    some = pl.ds(0, groups - 1)
    bulk = pltpu.make_async_remote_copy(
        src_ref=send_lev.at[some], dst_ref=recv_lev.at[some], send_sem=sems.at[2], recv_sem=sems.at[3],
        device_id={"lev": lax.rem(group + 1, groups)}, device_id_type=MESH,
    )
    bulk.wait()
    fetch.wait()
    left = jnp.concatenate([recv_lev[v].astype(jnp.float32) for v in range(groups)], axis=0).astype(jnp.bfloat16)
    first = (band * groups + group) * slot_dev
    width = 256
    for at in range(0, top_wave, width):
        slot = lax.broadcasted_iota(jnp.int32, (128, width), 0) % slot_dev
        order = lax.broadcasted_iota(jnp.int32, (128, width), 1) + at
        value = jnp.zeros((128, width), jnp.float32)
        for s in range(slot_dev):
            product = jnp.dot(left, leg_scr[s, :, at : at + width], preferred_element_type=jnp.float32)
            value = jnp.where((slot == s) & (order >= lane_wave_ref[first + s]), product, value)
        out_ref[:, at : at + width] = value.astype(jnp.bfloat16)


def transform_all(
    grid, below, above, donor, choice, kernels, lengths, slot_wave, legendre, bands, groups
):
    levels, blocks, lanes = grid.shape
    circles = blocks * lanes // PTS
    slots = slot_wave.shape[0]
    slot_dev, across, top_wave = legendre.shape
    share = 4 * slot_dev
    vmem = pl.BlockSpec(memory_space=pltpu.VMEM)
    smem = pl.BlockSpec(memory_space=pltpu.SMEM)
    waves = slot_wave.astype(jnp.float32).reshape(slots // CHUNK, 1, CHUNK)
    return pl.pallas_call(
        functools.partial(whole_kernel, top_wave, bands, groups, slot_dev),
        out_shape=jax.ShapeDtypeStruct((groups * share, top_wave), jnp.bfloat16),
        in_specs=[vmem] * 6 + [smem, vmem, smem, pl.BlockSpec(memory_space=pl.ANY)],
        out_specs=vmem,
        scratch_shapes=[
            pltpu.VMEM((blocks + 2 * below.shape[1], levels * lanes), jnp.bfloat16),
            pltpu.VMEM((kernels.shape[0], levels * lanes, levels * lanes), jnp.bfloat16),
            pltpu.VMEM((8, blocks), jnp.float32),
            pltpu.VMEM((circles, 96, lanes), jnp.bfloat16),
            pltpu.VMEM((circles, CHUNK), jnp.float32),
            pltpu.VMEM((4, circles, CHUNK), jnp.float32),
            pltpu.VMEM((bands, circles, 128), jnp.bfloat16),
            pltpu.VMEM((bands, circles, 128), jnp.bfloat16),
            pltpu.VMEM((groups, share, across), jnp.bfloat16),
            pltpu.VMEM((groups, share, across), jnp.bfloat16),
            pltpu.VMEM(legendre.shape, jnp.bfloat16),
            pltpu.SemaphoreType.DMA((4,)),
            pltpu.SemaphoreType.DMA,
        ],
        compiler_params=pltpu.CompilerParams(
            vmem_limit_bytes=40 * 1024 * 1024, collective_id=0, has_side_effects=True
        ),
        name="interpolate_transform_exchange",
    )(grid, below, above, donor, choice, kernels, lengths, waves, slot_wave, legendre)


def shift_bands(outgoing, cap):
    size = lax.axis_size("lat")
    up = [(i, i + 1) for i in range(size - 1)]
    down = [(j, i) for i, j in up]
    below = lax.ppermute(outgoing[:, cap:], "lat", up)
    above = lax.ppermute(outgoing[:, :cap], "lat", down)
    return below, above


def body(
    grid_field, send_blocks, donor_index, tile_choice, kernel_tiles, circle_len, slot_wave, legendre
):
    levels, blocks, lanes = grid_field.shape
    cap = send_blocks.shape[2]
    top_wave = legendre.shape[2]
    slot_dev = legendre.shape[0]
    bands = lax.axis_size("lat")
    level_groups = lax.axis_size("lev")
    outgoing = jnp.take(grid_field, send_blocks[0].reshape(-1), axis=1)
    below, above = shift_bands(outgoing, cap)
    spectra = transform_all(
        grid_field, below, above, donor_index.T, tile_choice.T, kernel_tiles, circle_len,
        slot_wave, legendre, bands, level_groups,
    )
    return spectra.reshape(level_groups * levels, 2, slot_dev, top_wave)


def solution(mesh):
    return jax.shard_map(
        body,
        mesh=mesh,
        in_specs=(
            P("lev", "lat", None),
            P("lat", None, None),
            P("lat", None),
            P("lat", None),
            P(),
            P(),
            P(),
            P(("lat", "lev"), None, None),
        ),
        out_specs=P(None, None, ("lat", "lev"), None),
        check_vma=False,
    )
```

```python
import functools

import jax
import jax.numpy as jnp
from jax import lax
from jax.experimental import pallas as pl
from jax.experimental.pallas import tpu as pltpu
from jax.sharding import PartitionSpec as P

PTS = 5120
FINE = 128
CHUNK = 256
PAIR = 8
EARLY = 4

SIN_COEF = (3.1415927410125732, -5.167709827423096, 2.550076961517334, -0.5982874631881714, 0.07764891535043716)
COS_COEF = (1.0, -4.934792518615723, 4.058409690856934, -1.331863284111023, 0.21965928375720978)


def poly(coef, x):
    acc = jnp.full_like(x, coef[-1])
    for c in coef[-2::-1]:
        acc = acc * x + c
    return acc


def phase(steps, length, inverse):
    turns = jnp.floor(steps * inverse + 0.5)
    u = (steps - turns * length) * inverse
    u2 = u * u
    s = u * poly(SIN_COEF, u2)
    c = poly(COS_COEF, u2)
    return 1.0 - 2.0 * s * s, -2.0 * s * c


def times(a, b):
    return a[0] * b[0] - a[1] * b[1], a[0] * b[1] + a[1] * b[0]


MESH = pl.DeviceIdType.MESH


def interpolate(band, len_ref, columns, pool_scr, diag_scr, x_scr):
    pool_size, width = pool_scr.shape
    tiles = diag_scr.shape[0]
    circles, _, lanes = x_scr.shape
    levels = width // lanes
    per_circle = columns.shape[0] // circles
    group = 4
    rows = group * per_circle
    for start in range(0, circles, group):
        part = columns[start * per_circle : (start + group) * per_circle, :]
        total = jnp.zeros((rows, width), jnp.float32)
        spots = lax.broadcasted_iota(jnp.int32, (rows, pool_size), 1).astype(jnp.float32)
        for k in range(2):
            hot = jnp.where(spots == part[:, k : k + 1], 1.0, 0.0).astype(jnp.bfloat16)
            picked = jnp.dot(hot, pool_scr[...], preferred_element_type=jnp.float32)
            which = part[:, 2 + k : 3 + k]
            for t in range(tiles):
                chosen = jnp.where(which == float(t), picked, 0.0).astype(jnp.bfloat16)
                total += jnp.dot(chosen, diag_scr[t], preferred_element_type=jnp.float32)
        squared = total * total
        for c in range(group):
            n = len_ref[band * circles + start + c]
            spot = lax.broadcasted_iota(jnp.int32, (per_circle, lanes), 0) * lanes
            spot = spot + lax.broadcasted_iota(jnp.int32, (per_circle, lanes), 1)
            for l in range(levels):
                piece = squared[c * per_circle : (c + 1) * per_circle, l * lanes : (l + 1) * lanes]
                piece = jnp.where(spot < n, piece, 0.0).astype(jnp.bfloat16)
                x_scr[start + c, 48 * l : 48 * l + per_circle, :] = piece


def circle_tables(g, chunk, wave, len_scr, table_scr, outer_scr):
    row = lax.broadcasted_iota(jnp.int32, (8, CHUNK), 0).astype(jnp.float32)
    wave_rows = row * wave
    length = len_scr[pl.ds(g, 1), :]
    inverse = 1.0 / length
    base = phase(wave_rows, length, inverse)
    outer = phase(wave_rows * float(FINE), length, inverse)
    outer_scr[chunk, g, 0:8, :] = outer[0]
    outer_scr[chunk, g, 8:16, :] = outer[1]
    step = times((base[0][7:8], base[1][7:8]), (base[0][1:2], base[1][1:2]))
    twice = jnp.broadcast_to(2.0 * step[0], base[0].shape)
    second = times(base, step)
    for part in range(2):
        rows = [base[part], second[part]]
        for q in range(2, FINE // 8):
            rows.append(twice * rows[-1] - rows[-2])
        table = jnp.concatenate(rows, axis=0).astype(jnp.bfloat16)
        table_scr[chunk, g, :, part * CHUNK : (part + 1) * CHUNK] = table


def transform_circle(g, chunk, wave, top_wave, levels, per_circle, x_scr, len_scr, table_scr, outer_scr, coef_scr):
    length = len_scr[pl.ds(g, 1), :]
    outer = (outer_scr[chunk, g, 0:8, :], outer_scr[chunk, g, 8:16, :])
    jump = times((outer[0][7:8], outer[1][7:8]), (outer[0][1:2], outer[1][1:2]))
    jump = (jnp.broadcast_to(jump[0], (8, CHUNK)), jnp.broadcast_to(jump[1], (8, CHUNK)))
    x = x_scr[g]
    real = jnp.dot(x, table_scr[chunk, g, :, :CHUNK], preferred_element_type=jnp.float32)
    imag = jnp.dot(x, table_scr[chunk, g, :, CHUNK:], preferred_element_type=jnp.float32)
    live = (wave >= 1.0) & (wave < float(top_wave)) & (2.0 * wave < length)
    for l in range(levels):
        last = per_circle // 8 - 1
        at = 48 * l + 8 * last
        total = (real[at : at + 8], imag[at : at + 8])
        for q in range(last - 1, -1, -1):
            at = 48 * l + 8 * q
            turned = times(total, jump)
            total = (turned[0] + real[at : at + 8], turned[1] + imag[at : at + 8])
        total = times(total, outer)
        for c in range(2):
            value = jnp.sum(total[c], axis=0, keepdims=True)
            coef_scr[2 * l + c, pl.ds(g, 1), :] = jnp.where(live, value, 0.0)


def pack_tiles(first, coef_scr, send_scr):
    circles = coef_scr.shape[1]
    quarter = lax.broadcasted_iota(jnp.int32, (circles, 128), 1) // 32
    for block in range(CHUNK // 128):
        parts = [coef_scr[k, :, block * 128 : (block + 1) * 128] for k in range(4)]
        for to in range(4):
            value = parts[to]
            for k in range(4):
                if k != to:
                    value = jnp.where(quarter == k, pltpu.roll(parts[k], (32 * (k - to)) % 128, 1), value)
            send_scr[first + block * 4 + to] = value.astype(jnp.bfloat16)


def whole_kernel(
    top_wave, bands, groups, slot_dev,
    grid_ref, send_ref, donor_ref, tile_ref, kern_ref, len_hbm, wave_hbm, wave_rows_ref, legendre_ref, out_ref,
    pool_scr, diag_scr, send_scr, donor_scr, tile_scr, idx_scr, halo_scr, len_ref, slot_ref, wave_scr, waves_scr,
    x_scr, len_scr, table_scr, outer_scr, coef_scr, send_lat, recv_lat, send_lev, recv_lev, leg_scr,
    sems, halo_sems, load_sems, leg_sem
):
    levels, blocks, lanes = grid_ref.shape
    cap = halo_scr.shape[1]
    circles = x_scr.shape[0]
    per_circle = blocks // circles
    band, group = lax.axis_index("lat"), lax.axis_index("lev")
    pairs = [(len_hbm, len_ref), (wave_rows_ref, wave_scr), (send_ref, send_scr), (donor_ref, donor_scr), (tile_ref, tile_scr)]
    for l in range(levels):
        cols = slice(l * lanes, (l + 1) * lanes)
        pairs.append((grid_ref.at[l], pool_scr.at[0:blocks, cols]))
    for l in range(levels):
        cols = slice(l * lanes, (l + 1) * lanes)
        pairs.append((kern_ref, diag_scr.at[:, cols, cols]))
    pairs.append((wave_hbm, slot_ref))
    loads = [pltpu.make_async_copy(src, dst, load_sems.at[i]) for i, (src, dst) in enumerate(pairs)]
    for load in loads:
        load.start()
    fetch = pltpu.make_async_copy(legendre_ref, leg_scr, leg_sem)
    fetch.start()
    barrier = pltpu.get_barrier_semaphore()

    def greet_lat(i, carry):
        pl.semaphore_signal(barrier, inc=1, device_id={"lat": lax.rem(band + i, bands)}, device_id_type=MESH)
        return carry

    def greet_lev(i, carry):
        pl.semaphore_signal(barrier, inc=1, device_id={"lev": lax.rem(group + i, groups)}, device_id_type=MESH)
        return carry

    lax.fori_loop(1, bands, greet_lat, 0)
    lax.fori_loop(1, groups, greet_lev, 0)

    for l in range(levels):
        for m in range(levels):
            if l != m:
                rows, cols = slice(l * lanes, (l + 1) * lanes), slice(m * lanes, (m + 1) * lanes)
                diag_scr[:, rows, cols] = jnp.zeros((diag_scr.shape[0], lanes, lanes), jnp.bfloat16)
    idx_scr[...] = jnp.zeros_like(idx_scr)

    @pl.when(band == 0)
    def _():
        pool_scr[blocks : blocks + cap, :] = jnp.zeros((cap, levels * lanes), jnp.bfloat16)

    @pl.when(band == bands - 1)
    def _():
        pool_scr[blocks + cap : blocks + 2 * cap, :] = jnp.zeros((cap, levels * lanes), jnp.bfloat16)

    loads[0].wait()
    loads[1].wait()
    for g in range(circles):
        n = len_ref[band * circles + g]
        len_scr[g : g + 1, :] = jnp.full((1, CHUNK), n, jnp.int32).astype(jnp.float32)
    chunks = waves_scr.shape[0]
    each = CHUNK // 128
    for chunk in range(chunks):
        for k in range(each):
            at = chunk * each + k
            waves_scr[chunk, :, k * 128 : (k + 1) * 128] = wave_scr[at : at + 1, :].astype(jnp.float32)

    def table_step(step, carry):
        wave = waves_scr[step // (circles // PAIR)]
        for k in range(PAIR):
            g = step % (circles // PAIR) * PAIR + k
            circle_tables(g, step // (circles // PAIR), wave, len_scr, table_scr, outer_scr)
        return carry

    ahead = chunks * EARLY // 6 * (circles // PAIR)
    lax.fori_loop(0, ahead, table_step, 0)

    for load in loads[2:]:
        load.wait()
    idx_scr[0:2, :] = donor_scr[...].astype(jnp.float32)
    idx_scr[2:4, :] = tile_scr[...].astype(jnp.float32)
    idx_scr[4:6, 0:cap] = send_scr[0].astype(jnp.float32)
    columns = idx_scr[...].T
    own = lax.broadcasted_iota(jnp.int32, (cap, blocks), 1).astype(jnp.float32)
    for side in range(2):
        hot = jnp.where(own == columns[0:cap, 4 + side : 5 + side], 1.0, 0.0).astype(jnp.bfloat16)
        rows = jnp.dot(hot, pool_scr[0:blocks, :], preferred_element_type=jnp.float32)
        halo_scr[side] = rows.astype(jnp.bfloat16)
    pl.semaphore_wait(barrier, bands + groups - 2)

    down = pltpu.make_async_remote_copy(
        src_ref=halo_scr.at[0], dst_ref=pool_scr.at[blocks + cap : blocks + 2 * cap], send_sem=halo_sems.at[0],
        recv_sem=halo_sems.at[1], device_id={"lat": lax.rem(band + bands - 1, bands)}, device_id_type=MESH,
    )
    up = pltpu.make_async_remote_copy(
        src_ref=halo_scr.at[1], dst_ref=pool_scr.at[blocks : blocks + cap], send_sem=halo_sems.at[2],
        recv_sem=halo_sems.at[3], device_id={"lat": lax.rem(band + 1, bands)}, device_id_type=MESH,
    )

    @pl.when(band > 0)
    def _():
        down.start()

    @pl.when(band < bands - 1)
    def _():
        up.start()

    lax.fori_loop(ahead, chunks * (circles // PAIR), table_step, 0)

    @pl.when(band > 0)
    def _():
        down.wait_send()
        up.wait_recv()

    @pl.when(band < bands - 1)
    def _():
        up.wait_send()
        down.wait_recv()

    interpolate(band, len_ref, columns, pool_scr, diag_scr, x_scr)

    per_chunk = bands // chunks

    def lat_copy(source, to):
        return pltpu.make_async_remote_copy(
            src_ref=send_lat.at[source], dst_ref=recv_lat.at[band], send_sem=sems.at[0], recv_sem=sems.at[1],
            device_id={"lat": to}, device_id_type=MESH,
        )

    def chunk_step(step, carry):
        chunk = lax.rem(step + band // per_chunk, chunks)
        wave = waves_scr[chunk]

        def circle(i, inner):
            for k in range(PAIR):
                transform_circle(
                    i * PAIR + k, chunk, wave, top_wave, levels, per_circle, x_scr, len_scr, table_scr, outer_scr, coef_scr
                )
            return inner

        lax.fori_loop(0, circles // PAIR, circle, 0)
        pack_tiles(chunk * per_chunk, coef_scr, send_lat)
        for i in range(per_chunk):
            to = chunk * per_chunk + i

            @pl.when(to != band)
            def _():
                lat_copy(to, to).start()

        return carry

    lax.fori_loop(0, chunks, chunk_step, 0)
    recv_lat[band] = send_lat[band]
    some = pl.ds(0, bands - 1)
    bulk = pltpu.make_async_remote_copy(
        src_ref=send_lat.at[some], dst_ref=recv_lat.at[some], send_sem=sems.at[0], recv_sem=sems.at[1],
        device_id={"lat": lax.rem(band + 1, bands)}, device_id_type=MESH,
    )
    bulk.wait()

    target = lax.broadcasted_iota(jnp.int32, (128, 128), 0)
    source = lax.broadcasted_iota(jnp.int32, (128, 128), 1)
    share = 4 * slot_dev
    wanted = (target % share) // slot_dev * (groups * slot_dev) + target // share * slot_dev + target % slot_dev
    pick = jnp.where(source == wanted, 1.0, 0.0).astype(jnp.bfloat16)
    arrived = recv_lat[...].reshape(bands * circles, 128)
    turned = lax.dot_general(pick, arrived, (((1,), (1,)), ((), ())), preferred_element_type=jnp.float32)
    for v in range(groups):
        send_lev[v] = turned[v * share : (v + 1) * share].astype(jnp.bfloat16)

    def send_group(i, carry):
        to = lax.rem(group + i, groups)
        pltpu.make_async_remote_copy(
            src_ref=send_lev.at[to], dst_ref=recv_lev.at[group], send_sem=sems.at[2], recv_sem=sems.at[3],
            device_id={"lev": to}, device_id_type=MESH,
        ).start()
        return carry

    lax.fori_loop(1, groups, send_group, 0)
    recv_lev[group] = send_lev[group]
    some = pl.ds(0, groups - 1)
    bulk = pltpu.make_async_remote_copy(
        src_ref=send_lev.at[some], dst_ref=recv_lev.at[some], send_sem=sems.at[2], recv_sem=sems.at[3],
        device_id={"lev": lax.rem(group + 1, groups)}, device_id_type=MESH,
    )
    bulk.wait()
    fetch.wait()
    left = jnp.concatenate([recv_lev[v].astype(jnp.float32) for v in range(groups)], axis=0).astype(jnp.bfloat16)
    first = (band * groups + group) * slot_dev
    width = 256
    for at in range(0, top_wave, width):
        slot = lax.broadcasted_iota(jnp.int32, (128, width), 0) % slot_dev
        order = lax.broadcasted_iota(jnp.int32, (128, width), 1) + at
        value = jnp.zeros((128, width), jnp.float32)
        for s in range(slot_dev):
            product = jnp.dot(left, leg_scr[s, :, at : at + width], preferred_element_type=jnp.float32)
            value = jnp.where((slot == s) & (order >= slot_ref[first + s]), product, value)
        out_ref[:, at : at + width] = value.astype(jnp.bfloat16)


def body(
    grid_field, send_blocks, donor_index, tile_choice, kernel_tiles, circle_len, slot_wave, legendre
):
    levels, blocks, lanes = grid_field.shape
    cap = send_blocks.shape[2]
    bands = lax.axis_size("lat")
    groups = lax.axis_size("lev")
    circles = blocks * lanes // PTS
    slots = slot_wave.shape[0]
    slot_dev, across, top_wave = legendre.shape
    share = 2 * levels * slot_dev
    tiles = kernel_tiles.shape[0]
    width = levels * lanes
    chunks = slots // CHUNK
    bf16, f32, i32 = jnp.bfloat16, jnp.float32, jnp.int32
    hbm = pl.BlockSpec(memory_space=pltpu.HBM)
    spectra = pl.pallas_call(
        functools.partial(whole_kernel, top_wave, bands, groups, slot_dev),
        out_shape=jax.ShapeDtypeStruct((groups * share, top_wave), bf16),
        in_specs=[hbm] * 9,
        out_specs=pl.BlockSpec(memory_space=pltpu.VMEM),
        scratch_shapes=[
            pltpu.VMEM((blocks + 2 * cap, width), bf16),
            pltpu.VMEM((tiles, width, width), bf16),
            pltpu.VMEM((1, 2, cap), i32),
            pltpu.VMEM((2, blocks), i32),
            pltpu.VMEM((2, blocks), i32),
            pltpu.VMEM((8, blocks), f32),
            pltpu.VMEM((2, cap, width), bf16),
            pltpu.SMEM(circle_len.shape, i32),
            pltpu.SMEM(slot_wave.shape, i32),
            pltpu.VMEM((slots // 128, 128), i32),
            pltpu.VMEM((chunks, 1, CHUNK), f32),
            pltpu.VMEM((circles, 96, lanes), bf16),
            pltpu.VMEM((circles, CHUNK), f32),
            pltpu.VMEM((chunks, circles, FINE, 2 * CHUNK), bf16),
            pltpu.VMEM((chunks, circles, 16, CHUNK), f32),
            pltpu.VMEM((2 * levels, circles, CHUNK), f32),
            pltpu.VMEM((bands, circles, 128), bf16),
            pltpu.VMEM((bands, circles, 128), bf16),
            pltpu.VMEM((groups, share, across), bf16),
            pltpu.VMEM((groups, share, across), bf16),
            pltpu.VMEM(legendre.shape, bf16),
            pltpu.SemaphoreType.DMA((4,)),
            pltpu.SemaphoreType.DMA((4,)),
            pltpu.SemaphoreType.DMA((10,)),
            pltpu.SemaphoreType.DMA,
        ],
        compiler_params=pltpu.CompilerParams(
            vmem_limit_bytes=56 * 1024 * 1024, collective_id=0, has_side_effects=True
        ),
        name="interpolate_transform_exchange",
    )(
        grid_field, send_blocks, donor_index.T, tile_choice.T, kernel_tiles, circle_len, slot_wave,
        slot_wave.reshape(slots // 128, 128), legendre,
    )
    return spectra.reshape(groups * levels, 2, slot_dev, top_wave)


def solution(mesh):
    return jax.shard_map(
        body,
        mesh=mesh,
        in_specs=(
            P("lev", "lat", None),
            P("lat", None, None),
            P("lat", None),
            P("lat", None),
            P(),
            P(),
            P(),
            P(("lat", "lev"), None, None),
        ),
        out_specs=P(None, None, ("lat", "lev"), None),
        check_vma=False,
    )
```

```python
import functools

import jax
import jax.numpy as jnp
from jax import lax
from jax.experimental import pallas as pl
from jax.experimental.pallas import tpu as pltpu
from jax.sharding import PartitionSpec as P

PTS = 5120
FINE = 128
CHUNK = 256
PAIR = 8
EARLY = 4

SIN_COEF = (3.1415927410125732, -5.167709827423096, 2.550076961517334, -0.5982874631881714, 0.07764891535043716)
COS_COEF = (1.0, -4.934792518615723, 4.058409690856934, -1.331863284111023, 0.21965928375720978)


def poly(coef, x):
    acc = jnp.full_like(x, coef[-1])
    for c in coef[-2::-1]:
        acc = acc * x + c
    return acc


def phase(steps, length, inverse):
    turns = jnp.floor(steps * inverse + 0.5)
    u = (steps - turns * length) * inverse
    u2 = u * u
    s = u * poly(SIN_COEF, u2)
    c = poly(COS_COEF, u2)
    return 1.0 - 2.0 * s * s, -2.0 * s * c


def times(a, b):
    return a[0] * b[0] - a[1] * b[1], a[0] * b[1] + a[1] * b[0]


MESH = pl.DeviceIdType.MESH


def interpolate(band, len_ref, columns, pool_scr, diag_scr, x_scr):
    pool_size, width = pool_scr.shape
    tiles = diag_scr.shape[0]
    circles, _, lanes = x_scr.shape
    levels = width // lanes
    per_circle = columns.shape[0] // circles
    group = 4
    rows = group * per_circle
    for start in range(0, circles, group):
        part = columns[start * per_circle : (start + group) * per_circle, :]
        total = jnp.zeros((rows, width), jnp.float32)
        spots = lax.broadcasted_iota(jnp.int32, (rows, pool_size), 1).astype(jnp.float32)
        for k in range(2):
            hot = jnp.where(spots == part[:, k : k + 1], 1.0, 0.0).astype(jnp.bfloat16)
            picked = jnp.dot(hot, pool_scr[...], preferred_element_type=jnp.float32)
            which = part[:, 2 + k : 3 + k]
            for t in range(tiles):
                chosen = jnp.where(which == float(t), picked, 0.0).astype(jnp.bfloat16)
                total += jnp.dot(chosen, diag_scr[t], preferred_element_type=jnp.float32)
        squared = total * total
        for c in range(group):
            n = len_ref[band * circles + start + c]
            spot = lax.broadcasted_iota(jnp.int32, (per_circle, lanes), 0) * lanes
            spot = spot + lax.broadcasted_iota(jnp.int32, (per_circle, lanes), 1)
            for l in range(levels):
                piece = squared[c * per_circle : (c + 1) * per_circle, l * lanes : (l + 1) * lanes]
                piece = jnp.where(spot < n, piece, 0.0).astype(jnp.bfloat16)
                x_scr[start + c, 48 * l : 48 * l + per_circle, :] = piece


def circle_tables(g, chunk, wave, len_scr, table_scr, outer_scr):
    row = lax.broadcasted_iota(jnp.int32, (8, CHUNK), 0).astype(jnp.float32)
    wave_rows = row * wave
    length = len_scr[pl.ds(g, 1), :]
    inverse = 1.0 / length
    base = phase(wave_rows, length, inverse)
    outer = phase(wave_rows * float(FINE), length, inverse)
    outer_scr[chunk, g, 0:8, :] = outer[0]
    outer_scr[chunk, g, 8:16, :] = outer[1]
    step = times((base[0][7:8], base[1][7:8]), (base[0][1:2], base[1][1:2]))
    twice = jnp.broadcast_to(2.0 * step[0], base[0].shape)
    second = times(base, step)
    for part in range(2):
        rows = [base[part], second[part]]
        for q in range(2, FINE // 8):
            rows.append(twice * rows[-1] - rows[-2])
        table = jnp.concatenate(rows, axis=0).astype(jnp.bfloat16)
        table_scr[chunk, g, :, part * CHUNK : (part + 1) * CHUNK] = table


def transform_circle(g, chunk, wave, top_wave, levels, per_circle, x_scr, len_scr, table_scr, outer_scr, coef_scr):
    length = len_scr[pl.ds(g, 1), :]
    outer = (outer_scr[chunk, g, 0:8, :], outer_scr[chunk, g, 8:16, :])
    jump = times((outer[0][7:8], outer[1][7:8]), (outer[0][1:2], outer[1][1:2]))
    jump = (jnp.broadcast_to(jump[0], (8, CHUNK)), jnp.broadcast_to(jump[1], (8, CHUNK)))
    x = x_scr[g]
    real = jnp.dot(x, table_scr[chunk, g, :, :CHUNK], preferred_element_type=jnp.float32)
    imag = jnp.dot(x, table_scr[chunk, g, :, CHUNK:], preferred_element_type=jnp.float32)
    live = (wave >= 1.0) & (wave < float(top_wave)) & (2.0 * wave < length)
    for l in range(levels):
        last = per_circle // 8 - 1
        at = 48 * l + 8 * last
        total = (real[at : at + 8], imag[at : at + 8])
        for q in range(last - 1, -1, -1):
            at = 48 * l + 8 * q
            turned = times(total, jump)
            total = (turned[0] + real[at : at + 8], turned[1] + imag[at : at + 8])
        total = times(total, outer)
        for c in range(2):
            value = jnp.sum(total[c], axis=0, keepdims=True)
            coef_scr[2 * l + c, pl.ds(g, 1), :] = jnp.where(live, value, 0.0)


def pack_tiles(first, coef_scr, send_scr):
    circles = coef_scr.shape[1]
    quarter = lax.broadcasted_iota(jnp.int32, (circles, 128), 1) // 32
    for block in range(CHUNK // 128):
        parts = [coef_scr[k, :, block * 128 : (block + 1) * 128] for k in range(4)]
        for to in range(4):
            value = parts[to]
            for k in range(4):
                if k != to:
                    value = jnp.where(quarter == k, pltpu.roll(parts[k], (32 * (k - to)) % 128, 1), value)
            send_scr[first + block * 4 + to] = value.astype(jnp.bfloat16)


def whole_kernel(
    top_wave, bands, groups, slot_dev,
    grid_ref, send_ref, donor_ref, tile_ref, kern_ref, len_hbm, wave_hbm, wave_rows_ref, legendre_ref, out_ref,
    pool_scr, diag_scr, send_scr, donor_scr, tile_scr, idx_scr, halo_scr, len_ref, slot_ref, wave_scr, waves_scr,
    x_scr, len_scr, table_scr, outer_scr, coef_scr, send_lat, recv_lat, send_lev, recv_lev, leg_scr,
    total_scr, sems, lat_sems, lev_sems, halo_sems, load_sems, leg_sems
):
    levels, blocks, lanes = grid_ref.shape
    cap = halo_scr.shape[1]
    circles = x_scr.shape[0]
    per_circle = blocks // circles
    band, group = lax.axis_index("lat"), lax.axis_index("lev")
    pairs = [(len_hbm, len_ref), (wave_rows_ref, wave_scr), (send_ref, send_scr), (donor_ref, donor_scr), (tile_ref, tile_scr)]
    for l in range(levels):
        cols = slice(l * lanes, (l + 1) * lanes)
        pairs.append((grid_ref.at[l], pool_scr.at[0:blocks, cols]))
    for l in range(levels):
        cols = slice(l * lanes, (l + 1) * lanes)
        pairs.append((kern_ref, diag_scr.at[:, cols, cols]))
    pairs.append((wave_hbm, slot_ref))
    loads = [pltpu.make_async_copy(src, dst, load_sems.at[i]) for i, (src, dst) in enumerate(pairs)]
    for load in loads:
        load.start()
    fetches = []
    for p in range(leg_scr.shape[0]):
        for k in range(slot_dev):
            rows = slice(p * leg_scr.shape[2], (p + 1) * leg_scr.shape[2])
            fetches.append(pltpu.make_async_copy(legendre_ref.at[k, rows], leg_scr.at[p, k], leg_sems.at[p, k]))
    for fetch in fetches:
        fetch.start()
    barrier = pltpu.get_barrier_semaphore()

    def greet_lat(i, carry):
        pl.semaphore_signal(barrier, inc=1, device_id={"lat": lax.rem(band + i, bands)}, device_id_type=MESH)
        return carry

    def greet_lev(i, carry):
        pl.semaphore_signal(barrier, inc=1, device_id={"lev": lax.rem(group + i, groups)}, device_id_type=MESH)
        return carry

    lax.fori_loop(1, bands, greet_lat, 0)
    lax.fori_loop(1, groups, greet_lev, 0)

    for l in range(levels):
        for m in range(levels):
            if l != m:
                rows, cols = slice(l * lanes, (l + 1) * lanes), slice(m * lanes, (m + 1) * lanes)
                diag_scr[:, rows, cols] = jnp.zeros((diag_scr.shape[0], lanes, lanes), jnp.bfloat16)
    idx_scr[...] = jnp.zeros_like(idx_scr)

    @pl.when(band == 0)
    def _():
        pool_scr[blocks : blocks + cap, :] = jnp.zeros((cap, levels * lanes), jnp.bfloat16)

    @pl.when(band == bands - 1)
    def _():
        pool_scr[blocks + cap : blocks + 2 * cap, :] = jnp.zeros((cap, levels * lanes), jnp.bfloat16)

    loads[0].wait()
    loads[1].wait()
    for g in range(circles):
        n = len_ref[band * circles + g]
        len_scr[g : g + 1, :] = jnp.full((1, CHUNK), n, jnp.int32).astype(jnp.float32)
    chunks = waves_scr.shape[0]
    each = CHUNK // 128
    for chunk in range(chunks):
        for k in range(each):
            at = chunk * each + k
            waves_scr[chunk, :, k * 128 : (k + 1) * 128] = wave_scr[at : at + 1, :].astype(jnp.float32)

    def table_step(step, carry):
        wave = waves_scr[step // (circles // PAIR)]
        for k in range(PAIR):
            g = step % (circles // PAIR) * PAIR + k
            circle_tables(g, step // (circles // PAIR), wave, len_scr, table_scr, outer_scr)
        return carry

    ahead = chunks * EARLY // 6 * (circles // PAIR)
    lax.fori_loop(0, ahead, table_step, 0)

    for load in loads[2:]:
        load.wait()
    idx_scr[0:2, :] = donor_scr[...].astype(jnp.float32)
    idx_scr[2:4, :] = tile_scr[...].astype(jnp.float32)
    idx_scr[4:6, 0:cap] = send_scr[0].astype(jnp.float32)
    columns = idx_scr[...].T
    own = lax.broadcasted_iota(jnp.int32, (cap, blocks), 1).astype(jnp.float32)
    for side in range(2):
        hot = jnp.where(own == columns[0:cap, 4 + side : 5 + side], 1.0, 0.0).astype(jnp.bfloat16)
        rows = jnp.dot(hot, pool_scr[0:blocks, :], preferred_element_type=jnp.float32)
        halo_scr[side] = rows.astype(jnp.bfloat16)
    pl.semaphore_wait(barrier, bands + groups - 2)

    down = pltpu.make_async_remote_copy(
        src_ref=halo_scr.at[0], dst_ref=pool_scr.at[blocks + cap : blocks + 2 * cap], send_sem=halo_sems.at[0],
        recv_sem=halo_sems.at[1], device_id={"lat": lax.rem(band + bands - 1, bands)}, device_id_type=MESH,
    )
    up = pltpu.make_async_remote_copy(
        src_ref=halo_scr.at[1], dst_ref=pool_scr.at[blocks : blocks + cap], send_sem=halo_sems.at[2],
        recv_sem=halo_sems.at[3], device_id={"lat": lax.rem(band + 1, bands)}, device_id_type=MESH,
    )

    @pl.when(band > 0)
    def _():
        down.start()

    @pl.when(band < bands - 1)
    def _():
        up.start()

    lax.fori_loop(ahead, chunks * (circles // PAIR), table_step, 0)

    @pl.when(band > 0)
    def _():
        down.wait_send()
        up.wait_recv()

    @pl.when(band < bands - 1)
    def _():
        up.wait_send()
        down.wait_recv()

    interpolate(band, len_ref, columns, pool_scr, diag_scr, x_scr)

    per_chunk = bands // chunks
    home = band // per_chunk

    def chunk_step(step, carry):
        chunk = lax.rem(step + home, chunks)
        wave = waves_scr[chunk]

        def circle(i, inner):
            for k in range(PAIR):
                transform_circle(
                    i * PAIR + k, chunk, wave, top_wave, levels, per_circle, x_scr, len_scr, table_scr, outer_scr, coef_scr
                )
            return inner

        lax.fori_loop(0, circles // PAIR, circle, 0)
        pack_tiles(chunk * per_chunk, coef_scr, send_lat)
        for i in range(per_chunk):
            to = chunk * per_chunk + i

            @pl.when(to != band)
            def _():
                pltpu.make_async_remote_copy(
                    src_ref=send_lat.at[to], dst_ref=recv_lat.at[band], send_sem=sems.at[0],
                    recv_sem=lat_sems.at[home], device_id={"lat": to}, device_id_type=MESH,
                ).start()

        return carry

    lax.fori_loop(0, chunks, chunk_step, 0)
    recv_lat[band] = send_lat[band]
    next_band = {"lat": lax.rem(band + 1, bands)}
    next_group = {"lev": lax.rem(group + 1, groups)}

    def lat_wait(start, count, sem):
        some = pl.ds(start, count)
        return pltpu.make_async_remote_copy(
            src_ref=send_lat.at[some], dst_ref=recv_lat.at[some], send_sem=sems.at[0], recv_sem=sem,
            device_id=next_band, device_id_type=MESH,
        )

    def lev_wait(src, dst, sem):
        return pltpu.make_async_remote_copy(
            src_ref=src, dst_ref=dst, send_sem=sems.at[1], recv_sem=sem, device_id=next_group, device_id_type=MESH,
        )

    target = lax.broadcasted_iota(jnp.int32, (128, 128), 0)
    source = lax.broadcasted_iota(jnp.int32, (128, 128), 1)
    share = 4 * slot_dev
    wanted = (target % share) // slot_dev * (groups * slot_dev) + target // share * slot_dev + target % slot_dev
    pick = jnp.where(source == wanted, 1.0, 0.0).astype(jnp.bfloat16)
    span = per_chunk * circles
    for p in range(chunks):
        part = lax.rem(home + chunks - p, chunks)
        lat_wait(part * per_chunk, per_chunk - (p == 0), lat_sems.at[part]).wait_recv()
        arrived = recv_lat[pl.ds(part * per_chunk, per_chunk)].reshape(span, 128)
        turned = lax.dot_general(pick, arrived, (((1,), (1,)), ((), ())), preferred_element_type=jnp.float32)
        for v in range(groups):
            send_lev[p, v] = turned[v * share : (v + 1) * share].astype(jnp.bfloat16)

        def send_group(i, carry):
            to = lax.rem(group + i, groups)
            pltpu.make_async_remote_copy(
                src_ref=send_lev.at[p, to], dst_ref=recv_lev.at[p, group], send_sem=sems.at[1],
                recv_sem=lev_sems.at[p], device_id={"lev": to}, device_id_type=MESH,
            ).start()
            return carry

        lax.fori_loop(1, groups, send_group, 0)
        recv_lev[p, group] = send_lev[p, group]

    for fetch in fetches:
        fetch.wait()
    first = (band * groups + group) * slot_dev
    width = 256
    kinds = lax.broadcasted_iota(jnp.int32, (128, span), 0) % slot_dev
    for p in range(chunks):
        part = lax.rem(home + chunks - p, chunks)
        some = pl.ds(0, groups - 1)
        lev_wait(send_lev.at[p, some], recv_lev.at[p, some], lev_sems.at[p]).wait_recv()
        left = jnp.concatenate([recv_lev[p, v].astype(jnp.float32) for v in range(groups)], axis=0)
        left = jnp.concatenate([jnp.where(kinds == s, left, 0.0) for s in range(slot_dev)], axis=1).astype(jnp.bfloat16)
        for at in range(0, top_wave, width):
            cols = slice(at, at + width)
            right = leg_scr[part, :, :, cols].reshape(slot_dev * span, width)
            value = jnp.dot(left, right, preferred_element_type=jnp.float32)
            if p > 0:
                value = value + total_scr[:, cols]
            if p < chunks - 1:
                total_scr[:, cols] = value
                continue
            slot = lax.broadcasted_iota(jnp.int32, (128, width), 0) % slot_dev
            order = lax.broadcasted_iota(jnp.int32, (128, width), 1) + at
            least = jnp.zeros((128, width), jnp.int32)
            for s in range(slot_dev):
                least = jnp.where(slot == s, slot_ref[first + s], least)
            out_ref[:, cols] = jnp.where(order >= least, value, 0.0).astype(jnp.bfloat16)
    lat_wait(0, bands - 1, lat_sems.at[0]).wait_send()
    for p in range(chunks):
        some = pl.ds(0, groups - 1)
        lev_wait(send_lev.at[p, some], recv_lev.at[p, some], lev_sems.at[p]).wait_send()


def body(
    grid_field, send_blocks, donor_index, tile_choice, kernel_tiles, circle_len, slot_wave, legendre
):
    levels, blocks, lanes = grid_field.shape
    cap = send_blocks.shape[2]
    bands = lax.axis_size("lat")
    groups = lax.axis_size("lev")
    circles = blocks * lanes // PTS
    slots = slot_wave.shape[0]
    slot_dev, across, top_wave = legendre.shape
    share = 2 * levels * slot_dev
    tiles = kernel_tiles.shape[0]
    width = levels * lanes
    chunks = slots // CHUNK
    bf16, f32, i32 = jnp.bfloat16, jnp.float32, jnp.int32
    hbm = pl.BlockSpec(memory_space=pltpu.HBM)
    spectra = pl.pallas_call(
        functools.partial(whole_kernel, top_wave, bands, groups, slot_dev),
        out_shape=jax.ShapeDtypeStruct((groups * share, top_wave), bf16),
        in_specs=[hbm] * 9,
        out_specs=pl.BlockSpec(memory_space=pltpu.VMEM),
        scratch_shapes=[
            pltpu.VMEM((blocks + 2 * cap, width), bf16),
            pltpu.VMEM((tiles, width, width), bf16),
            pltpu.VMEM((1, 2, cap), i32),
            pltpu.VMEM((2, blocks), i32),
            pltpu.VMEM((2, blocks), i32),
            pltpu.VMEM((8, blocks), f32),
            pltpu.VMEM((2, cap, width), bf16),
            pltpu.SMEM(circle_len.shape, i32),
            pltpu.SMEM(slot_wave.shape, i32),
            pltpu.VMEM((slots // 128, 128), i32),
            pltpu.VMEM((chunks, 1, CHUNK), f32),
            pltpu.VMEM((circles, 96, lanes), bf16),
            pltpu.VMEM((circles, CHUNK), f32),
            pltpu.VMEM((chunks, circles, FINE, 2 * CHUNK), bf16),
            pltpu.VMEM((chunks, circles, 16, CHUNK), f32),
            pltpu.VMEM((2 * levels, circles, CHUNK), f32),
            pltpu.VMEM((bands, circles, 128), bf16),
            pltpu.VMEM((bands, circles, 128), bf16),
            pltpu.VMEM((chunks, groups, share, across // chunks), bf16),
            pltpu.VMEM((chunks, groups, share, across // chunks), bf16),
            pltpu.VMEM((chunks, slot_dev, across // chunks, top_wave), bf16),
            pltpu.VMEM((groups * share, top_wave), f32),
            pltpu.SemaphoreType.DMA((2,)),
            pltpu.SemaphoreType.DMA((chunks,)),
            pltpu.SemaphoreType.DMA((chunks,)),
            pltpu.SemaphoreType.DMA((4,)),
            pltpu.SemaphoreType.DMA((10,)),
            pltpu.SemaphoreType.DMA((chunks, slot_dev)),
        ],
        compiler_params=pltpu.CompilerParams(
            vmem_limit_bytes=56 * 1024 * 1024, collective_id=0, has_side_effects=True
        ),
        name="interpolate_transform_exchange",
    )(
        grid_field, send_blocks, donor_index.T, tile_choice.T, kernel_tiles, circle_len, slot_wave,
        slot_wave.reshape(slots // 128, 128), legendre,
    )
    return spectra.reshape(groups * levels, 2, slot_dev, top_wave)


def solution(mesh):
    return jax.shard_map(
        body,
        mesh=mesh,
        in_specs=(
            P("lev", "lat", None),
            P("lat", None, None),
            P("lat", None),
            P("lat", None),
            P(),
            P(),
            P(),
            P(("lat", "lev"), None, None),
        ),
        out_specs=P(None, None, ("lat", "lev"), None),
        check_vma=False,
    )
```

```python
import functools

import jax
import jax.numpy as jnp
from jax import lax
from jax.experimental import pallas as pl
from jax.experimental.pallas import tpu as pltpu
from jax.sharding import PartitionSpec as P

PTS = 5120
FINE = 128
CHUNK = 256
PAIR = 8
EARLY = 4

SIN_COEF = (3.1415927410125732, -5.167709827423096, 2.550076961517334, -0.5982874631881714, 0.07764891535043716)
COS_COEF = (1.0, -4.934792518615723, 4.058409690856934, -1.331863284111023, 0.21965928375720978)


def poly(coef, x):
    acc = jnp.full_like(x, coef[-1])
    for c in coef[-2::-1]:
        acc = acc * x + c
    return acc


def phase(steps, length, inverse):
    turns = jnp.floor(steps * inverse + 0.5)
    u = (steps - turns * length) * inverse
    u2 = u * u
    s = u * poly(SIN_COEF, u2)
    c = poly(COS_COEF, u2)
    return 1.0 - 2.0 * s * s, -2.0 * s * c


def times(a, b):
    return a[0] * b[0] - a[1] * b[1], a[0] * b[1] + a[1] * b[0]


MESH = pl.DeviceIdType.MESH


def interpolate(band, len_ref, columns, pool_scr, diag_scr, x_scr):
    pool_size, width = pool_scr.shape
    tiles = diag_scr.shape[0]
    circles, _, lanes = x_scr.shape
    levels = width // lanes
    per_circle = columns.shape[0] // circles
    group = 4
    rows = group * per_circle
    for start in range(0, circles, group):
        part = columns[start * per_circle : (start + group) * per_circle, :]
        total = jnp.zeros((rows, width), jnp.float32)
        spots = lax.broadcasted_iota(jnp.int32, (rows, pool_size), 1).astype(jnp.float32)
        for k in range(2):
            hot = jnp.where(spots == part[:, k : k + 1], 1.0, 0.0).astype(jnp.bfloat16)
            picked = jnp.dot(hot, pool_scr[...], preferred_element_type=jnp.float32)
            which = part[:, 2 + k : 3 + k]
            chosen = [jnp.where(which == float(t), picked, 0.0).astype(jnp.bfloat16) for t in range(tiles)]
            chosen = jnp.concatenate(chosen, axis=1)
            total += jnp.dot(chosen, diag_scr[...].reshape(tiles * width, width), preferred_element_type=jnp.float32)
        squared = total * total
        for c in range(group):
            n = len_ref[band * circles + start + c]
            spot = lax.broadcasted_iota(jnp.int32, (per_circle, lanes), 0) * lanes
            spot = spot + lax.broadcasted_iota(jnp.int32, (per_circle, lanes), 1)
            for l in range(levels):
                piece = squared[c * per_circle : (c + 1) * per_circle, l * lanes : (l + 1) * lanes]
                piece = jnp.where(spot < n, piece, 0.0).astype(jnp.bfloat16)
                x_scr[start + c, 48 * l : 48 * l + per_circle, :] = piece


def circle_tables(g, chunk, wave, len_scr, table_scr, outer_scr):
    row = lax.broadcasted_iota(jnp.int32, (8, CHUNK), 0).astype(jnp.float32)
    wave_rows = row * wave
    length = len_scr[pl.ds(g, 1), :]
    inverse = 1.0 / length
    base = phase(wave_rows, length, inverse)
    outer = phase(wave_rows * float(FINE), length, inverse)
    outer_scr[chunk, g, 0:8, :] = outer[0]
    outer_scr[chunk, g, 8:16, :] = outer[1]
    step = times((base[0][7:8], base[1][7:8]), (base[0][1:2], base[1][1:2]))
    twice = jnp.broadcast_to(2.0 * step[0], base[0].shape)
    second = times(base, step)
    for part in range(2):
        rows = [base[part], second[part]]
        for q in range(2, FINE // 8):
            rows.append(twice * rows[-1] - rows[-2])
        table = jnp.concatenate(rows, axis=0).astype(jnp.bfloat16)
        table_scr[chunk, g, :, part * CHUNK : (part + 1) * CHUNK] = table


def transform_circle(g, chunk, levels, per_circle, x_scr, table_scr, outer_scr, coef_scr):
    outer = (outer_scr[chunk, g, 0:8, :], outer_scr[chunk, g, 8:16, :])
    jump = times((outer[0][7:8], outer[1][7:8]), (outer[0][1:2], outer[1][1:2]))
    jump = (jnp.broadcast_to(jump[0], (8, CHUNK)), jnp.broadcast_to(jump[1], (8, CHUNK)))
    x = x_scr[g]
    real = jnp.dot(x, table_scr[chunk, g, :, :CHUNK], preferred_element_type=jnp.float32)
    imag = jnp.dot(x, table_scr[chunk, g, :, CHUNK:], preferred_element_type=jnp.float32)
    for l in range(levels):
        last = per_circle // 8 - 1
        at = 48 * l + 8 * last
        total = (real[at : at + 8], imag[at : at + 8])
        for q in range(last - 1, -1, -1):
            at = 48 * l + 8 * q
            turned = times(total, jump)
            total = (turned[0] + real[at : at + 8], turned[1] + imag[at : at + 8])
        total = times(total, outer)
        for c in range(2):
            for block in range(CHUNK // 128):
                coef_scr[2 * l + c, block, 8 * g : 8 * g + 8, :] = total[c][:, block * 128 : (block + 1) * 128]


def pack_tiles(first, wave, top_wave, len_scr, coef_scr, send_scr):
    circles = len_scr.shape[0]
    quarter = lax.broadcasted_iota(jnp.int32, (circles, 128), 1) // 32
    for block in range(CHUNK // 128):
        cols = slice(block * 128, (block + 1) * 128)
        waves = wave[:, cols]
        live = (waves >= 1.0) & (waves < float(top_wave)) & (2.0 * waves < len_scr[:, cols])
        parts = []
        for k in range(4):
            rows = [coef_scr[k, block, pl.ds(r, circles, stride=8), :] for r in range(8)]
            while len(rows) > 1:
                rows = [rows[i] + rows[i + 1] for i in range(0, len(rows), 2)]
            parts.append(jnp.where(live, rows[0], 0.0))
        for to in range(4):
            value = parts[to]
            for k in range(4):
                if k != to:
                    value = jnp.where(quarter == k, pltpu.roll(parts[k], (32 * (k - to)) % 128, 1), value)
            send_scr[first + block * 4 + to] = value.astype(jnp.bfloat16)


def whole_kernel(
    top_wave, bands, groups, slot_dev,
    grid_ref, send_ref, donor_ref, tile_ref, kern_ref, len_hbm, wave_hbm, wave_rows_ref, legendre_ref, out_ref,
    pool_scr, diag_scr, send_scr, donor_scr, tile_scr, idx_scr, halo_scr, len_ref, slot_ref, wave_scr, waves_scr,
    x_scr, len_scr, table_scr, outer_scr, coef_scr, send_lat, recv_lat, send_lev, recv_lev, leg_scr,
    total_scr, sems, lat_sems, lev_sems, halo_sems, load_sems, leg_sems
):
    levels, blocks, lanes = grid_ref.shape
    cap = halo_scr.shape[1]
    circles = x_scr.shape[0]
    per_circle = blocks // circles
    band, group = lax.axis_index("lat"), lax.axis_index("lev")
    pairs = [(len_hbm, len_ref), (wave_rows_ref, wave_scr), (send_ref, send_scr), (donor_ref, donor_scr), (tile_ref, tile_scr)]
    for l in range(levels):
        cols = slice(l * lanes, (l + 1) * lanes)
        pairs.append((grid_ref.at[l], pool_scr.at[0:blocks, cols]))
    for l in range(levels):
        cols = slice(l * lanes, (l + 1) * lanes)
        pairs.append((kern_ref, diag_scr.at[:, cols, cols]))
    pairs.append((wave_hbm, slot_ref))
    loads = [pltpu.make_async_copy(src, dst, load_sems.at[i]) for i, (src, dst) in enumerate(pairs)]
    for load in loads:
        load.start()
    fetches = []
    for p in range(leg_scr.shape[0]):
        for k in range(slot_dev):
            rows = slice(p * leg_scr.shape[2], (p + 1) * leg_scr.shape[2])
            fetches.append(pltpu.make_async_copy(legendre_ref.at[k, rows], leg_scr.at[p, k], leg_sems.at[p, k]))
    for fetch in fetches:
        fetch.start()
    barrier = pltpu.get_barrier_semaphore()

    def greet_lat(i, carry):
        pl.semaphore_signal(barrier, inc=1, device_id={"lat": lax.rem(band + i, bands)}, device_id_type=MESH)
        return carry

    def greet_lev(i, carry):
        pl.semaphore_signal(barrier, inc=1, device_id={"lev": lax.rem(group + i, groups)}, device_id_type=MESH)
        return carry

    lax.fori_loop(1, bands, greet_lat, 0)
    lax.fori_loop(1, groups, greet_lev, 0)

    for l in range(levels):
        for m in range(levels):
            if l != m:
                rows, cols = slice(l * lanes, (l + 1) * lanes), slice(m * lanes, (m + 1) * lanes)
                diag_scr[:, rows, cols] = jnp.zeros((diag_scr.shape[0], lanes, lanes), jnp.bfloat16)
    idx_scr[...] = jnp.zeros_like(idx_scr)

    @pl.when(band == 0)
    def _():
        pool_scr[blocks : blocks + cap, :] = jnp.zeros((cap, levels * lanes), jnp.bfloat16)

    @pl.when(band == bands - 1)
    def _():
        pool_scr[blocks + cap : blocks + 2 * cap, :] = jnp.zeros((cap, levels * lanes), jnp.bfloat16)

    loads[0].wait()
    loads[1].wait()
    for g in range(circles):
        n = len_ref[band * circles + g]
        len_scr[g : g + 1, :] = jnp.full((1, CHUNK), n, jnp.int32).astype(jnp.float32)
    chunks = waves_scr.shape[0]
    each = CHUNK // 128
    for chunk in range(chunks):
        for k in range(each):
            at = chunk * each + k
            waves_scr[chunk, :, k * 128 : (k + 1) * 128] = wave_scr[at : at + 1, :].astype(jnp.float32)

    def table_step(step, carry):
        wave = waves_scr[step // (circles // PAIR)]
        for k in range(PAIR):
            g = step % (circles // PAIR) * PAIR + k
            circle_tables(g, step // (circles // PAIR), wave, len_scr, table_scr, outer_scr)
        return carry

    ahead = chunks * EARLY // 6 * (circles // PAIR)
    lax.fori_loop(0, ahead, table_step, 0)

    for load in loads[2:]:
        load.wait()
    idx_scr[0:2, :] = donor_scr[...].astype(jnp.float32)
    idx_scr[2:4, :] = tile_scr[...].astype(jnp.float32)
    idx_scr[4:6, 0:cap] = send_scr[0].astype(jnp.float32)
    columns = idx_scr[...].T
    own = lax.broadcasted_iota(jnp.int32, (cap, blocks), 1).astype(jnp.float32)
    for side in range(2):
        hot = jnp.where(own == columns[0:cap, 4 + side : 5 + side], 1.0, 0.0).astype(jnp.bfloat16)
        rows = jnp.dot(hot, pool_scr[0:blocks, :], preferred_element_type=jnp.float32)
        halo_scr[side] = rows.astype(jnp.bfloat16)
    pl.semaphore_wait(barrier, bands + groups - 2)

    down = pltpu.make_async_remote_copy(
        src_ref=halo_scr.at[0], dst_ref=pool_scr.at[blocks + cap : blocks + 2 * cap], send_sem=halo_sems.at[0],
        recv_sem=halo_sems.at[1], device_id={"lat": lax.rem(band + bands - 1, bands)}, device_id_type=MESH,
    )
    up = pltpu.make_async_remote_copy(
        src_ref=halo_scr.at[1], dst_ref=pool_scr.at[blocks : blocks + cap], send_sem=halo_sems.at[2],
        recv_sem=halo_sems.at[3], device_id={"lat": lax.rem(band + 1, bands)}, device_id_type=MESH,
    )

    @pl.when(band > 0)
    def _():
        down.start()

    @pl.when(band < bands - 1)
    def _():
        up.start()

    lax.fori_loop(ahead, chunks * (circles // PAIR), table_step, 0)

    @pl.when(band > 0)
    def _():
        down.wait_send()
        up.wait_recv()

    @pl.when(band < bands - 1)
    def _():
        up.wait_send()
        down.wait_recv()

    interpolate(band, len_ref, columns, pool_scr, diag_scr, x_scr)

    per_chunk = bands // chunks
    home = band // per_chunk

    def chunk_step(step, carry):
        chunk = lax.rem(step + home, chunks)
        wave = waves_scr[chunk]

        for g in range(circles):
            transform_circle(g, chunk, levels, per_circle, x_scr, table_scr, outer_scr, coef_scr)
        pack_tiles(chunk * per_chunk, wave, top_wave, len_scr, coef_scr, send_lat)
        for i in range(per_chunk):
            to = chunk * per_chunk + i

            @pl.when(to != band)
            def _():
                pltpu.make_async_remote_copy(
                    src_ref=send_lat.at[to], dst_ref=recv_lat.at[band], send_sem=sems.at[0],
                    recv_sem=lat_sems.at[home], device_id={"lat": to}, device_id_type=MESH,
                ).start()

        return carry

    lax.fori_loop(0, chunks, chunk_step, 0)
    recv_lat[band] = send_lat[band]
    next_band = {"lat": lax.rem(band + 1, bands)}
    next_group = {"lev": lax.rem(group + 1, groups)}

    def lat_wait(start, count, sem):
        some = pl.ds(start, count)
        return pltpu.make_async_remote_copy(
            src_ref=send_lat.at[some], dst_ref=recv_lat.at[some], send_sem=sems.at[0], recv_sem=sem,
            device_id=next_band, device_id_type=MESH,
        )

    def lev_wait(src, dst, sem):
        return pltpu.make_async_remote_copy(
            src_ref=src, dst_ref=dst, send_sem=sems.at[1], recv_sem=sem, device_id=next_group, device_id_type=MESH,
        )

    target = lax.broadcasted_iota(jnp.int32, (128, 128), 0)
    source = lax.broadcasted_iota(jnp.int32, (128, 128), 1)
    share = 4 * slot_dev
    wanted = (target % share) // slot_dev * (groups * slot_dev) + target // share * slot_dev + target % slot_dev
    pick = jnp.where(source == wanted, 1.0, 0.0).astype(jnp.bfloat16)
    span = per_chunk * circles
    for p in range(chunks):
        part = lax.rem(home + chunks - p, chunks)
        lat_wait(part * per_chunk, per_chunk - (p == 0), lat_sems.at[part]).wait_recv()
        arrived = recv_lat[pl.ds(part * per_chunk, per_chunk)].reshape(span, 128)
        turned = lax.dot_general(pick, arrived, (((1,), (1,)), ((), ())), preferred_element_type=jnp.float32)
        for v in range(groups):
            send_lev[p, v] = turned[v * share : (v + 1) * share].astype(jnp.bfloat16)

        def send_group(i, carry):
            to = lax.rem(group + i, groups)
            pltpu.make_async_remote_copy(
                src_ref=send_lev.at[p, to], dst_ref=recv_lev.at[p, group], send_sem=sems.at[1],
                recv_sem=lev_sems.at[p], device_id={"lev": to}, device_id_type=MESH,
            ).start()
            return carry

        lax.fori_loop(1, groups, send_group, 0)
        recv_lev[p, group] = send_lev[p, group]

    for fetch in fetches:
        fetch.wait()
    first = (band * groups + group) * slot_dev
    width = 256
    kinds = lax.broadcasted_iota(jnp.int32, (128, span), 0) % slot_dev
    for p in range(chunks):
        part = lax.rem(home + chunks - p, chunks)
        some = pl.ds(0, groups - 1)
        lev_wait(send_lev.at[p, some], recv_lev.at[p, some], lev_sems.at[p]).wait_recv()
        left = jnp.concatenate([recv_lev[p, v].astype(jnp.float32) for v in range(groups)], axis=0)
        left = jnp.concatenate([jnp.where(kinds == s, left, 0.0) for s in range(slot_dev)], axis=1).astype(jnp.bfloat16)
        for at in range(0, top_wave, width):
            cols = slice(at, at + width)
            right = leg_scr[part, :, :, cols].reshape(slot_dev * span, width)
            value = jnp.dot(left, right, preferred_element_type=jnp.float32)
            if p > 0:
                value = value + total_scr[:, cols]
            if p < chunks - 1:
                total_scr[:, cols] = value
                continue
            slot = lax.broadcasted_iota(jnp.int32, (128, width), 0) % slot_dev
            order = lax.broadcasted_iota(jnp.int32, (128, width), 1) + at
            least = jnp.zeros((128, width), jnp.int32)
            for s in range(slot_dev):
                least = jnp.where(slot == s, slot_ref[first + s], least)
            out_ref[:, cols] = jnp.where(order >= least, value, 0.0).astype(jnp.bfloat16)
    lat_wait(0, bands - 1, lat_sems.at[0]).wait_send()
    for p in range(chunks):
        some = pl.ds(0, groups - 1)
        lev_wait(send_lev.at[p, some], recv_lev.at[p, some], lev_sems.at[p]).wait_send()


def body(
    grid_field, send_blocks, donor_index, tile_choice, kernel_tiles, circle_len, slot_wave, legendre
):
    levels, blocks, lanes = grid_field.shape
    cap = send_blocks.shape[2]
    bands = lax.axis_size("lat")
    groups = lax.axis_size("lev")
    circles = blocks * lanes // PTS
    slots = slot_wave.shape[0]
    slot_dev, across, top_wave = legendre.shape
    share = 2 * levels * slot_dev
    tiles = kernel_tiles.shape[0]
    width = levels * lanes
    chunks = slots // CHUNK
    bf16, f32, i32 = jnp.bfloat16, jnp.float32, jnp.int32
    hbm = pl.BlockSpec(memory_space=pltpu.HBM)
    spectra = pl.pallas_call(
        functools.partial(whole_kernel, top_wave, bands, groups, slot_dev),
        out_shape=jax.ShapeDtypeStruct((groups * share, top_wave), bf16),
        in_specs=[hbm] * 9,
        out_specs=pl.BlockSpec(memory_space=pltpu.VMEM),
        scratch_shapes=[
            pltpu.VMEM((blocks + 2 * cap, width), bf16),
            pltpu.VMEM((tiles, width, width), bf16),
            pltpu.VMEM((1, 2, cap), i32),
            pltpu.VMEM((2, blocks), i32),
            pltpu.VMEM((2, blocks), i32),
            pltpu.VMEM((8, blocks), f32),
            pltpu.VMEM((2, cap, width), bf16),
            pltpu.SMEM(circle_len.shape, i32),
            pltpu.SMEM(slot_wave.shape, i32),
            pltpu.VMEM((slots // 128, 128), i32),
            pltpu.VMEM((chunks, 1, CHUNK), f32),
            pltpu.VMEM((circles, 96, lanes), bf16),
            pltpu.VMEM((circles, CHUNK), f32),
            pltpu.VMEM((chunks, circles, FINE, 2 * CHUNK), bf16),
            pltpu.VMEM((chunks, circles, 16, CHUNK), f32),
            pltpu.VMEM((2 * levels, CHUNK // 128, 8 * circles, 128), f32),
            pltpu.VMEM((bands, circles, 128), bf16),
            pltpu.VMEM((bands, circles, 128), bf16),
            pltpu.VMEM((chunks, groups, share, across // chunks), bf16),
            pltpu.VMEM((chunks, groups, share, across // chunks), bf16),
            pltpu.VMEM((chunks, slot_dev, across // chunks, top_wave), bf16),
            pltpu.VMEM((groups * share, top_wave), f32),
            pltpu.SemaphoreType.DMA((2,)),
            pltpu.SemaphoreType.DMA((chunks,)),
            pltpu.SemaphoreType.DMA((chunks,)),
            pltpu.SemaphoreType.DMA((4,)),
            pltpu.SemaphoreType.DMA((10,)),
            pltpu.SemaphoreType.DMA((chunks, slot_dev)),
        ],
        compiler_params=pltpu.CompilerParams(
            vmem_limit_bytes=40 * 1024 * 1024, collective_id=0, has_side_effects=True
        ),
        name="interpolate_transform_exchange",
    )(
        *(
            pltpu.with_memory_space_constraint(array, pltpu.HBM)
            for array in (
                grid_field, send_blocks, donor_index.T, tile_choice.T, kernel_tiles, circle_len, slot_wave,
                slot_wave.reshape(slots // 128, 128), legendre,
            )
        )
    )
    return spectra.reshape(groups * levels, 2, slot_dev, top_wave)


def solution(mesh):
    return jax.shard_map(
        body,
        mesh=mesh,
        in_specs=(
            P("lev", "lat", None),
            P("lat", None, None),
            P("lat", None),
            P("lat", None),
            P(),
            P(),
            P(),
            P(("lat", "lev"), None, None),
        ),
        out_specs=P(None, None, ("lat", "lev"), None),
        check_vma=False,
    )
```

```python
import functools

import jax
import jax.numpy as jnp
from jax import lax
from jax.experimental import pallas as pl
from jax.experimental.pallas import tpu as pltpu
from jax.sharding import PartitionSpec as P

PTS = 5120
FINE = 128
CHUNK = 256
PAIR = 8
EARLY = 6

SIN_COEF = (3.1415927410125732, -5.167709827423096, 2.550076961517334, -0.5982874631881714, 0.07764891535043716)
COS_COEF = (1.0, -4.934792518615723, 4.058409690856934, -1.331863284111023, 0.21965928375720978)


def poly(coef, x):
    acc = jnp.full_like(x, coef[-1])
    for c in coef[-2::-1]:
        acc = acc * x + c
    return acc


def phase(steps, length, inverse):
    turns = jnp.floor(steps * inverse + 0.5)
    u = (steps - turns * length) * inverse
    u2 = u * u
    s = u * poly(SIN_COEF, u2)
    c = poly(COS_COEF, u2)
    return 1.0 - 2.0 * s * s, -2.0 * s * c


def times(a, b):
    return a[0] * b[0] - a[1] * b[1], a[0] * b[1] + a[1] * b[0]


MESH = pl.DeviceIdType.MESH


def interpolate(band, len_ref, columns, pool_scr, diag_scr, x_scr):
    pool_size, width = pool_scr.shape
    tiles = diag_scr.shape[0]
    circles, _, lanes = x_scr.shape
    levels = width // lanes
    per_circle = columns.shape[0] // circles
    group = 4
    rows = group * per_circle
    for start in range(0, circles, group):
        part = columns[start * per_circle : (start + group) * per_circle, :]
        total = jnp.zeros((rows, width), jnp.float32)
        spots = lax.broadcasted_iota(jnp.int32, (rows, pool_size), 1).astype(jnp.float32)
        for k in range(2):
            hot = jnp.where(spots == part[:, k : k + 1], 1.0, 0.0).astype(jnp.bfloat16)
            picked = jnp.dot(hot, pool_scr[...], preferred_element_type=jnp.float32)
            which = part[:, 2 + k : 3 + k]
            chosen = [jnp.where(which == float(t), picked, 0.0).astype(jnp.bfloat16) for t in range(tiles)]
            chosen = jnp.concatenate(chosen, axis=1)
            total += jnp.dot(chosen, diag_scr[...].reshape(tiles * width, width), preferred_element_type=jnp.float32)
        squared = total * total
        for c in range(group):
            n = len_ref[band * circles + start + c]
            spot = lax.broadcasted_iota(jnp.int32, (per_circle, lanes), 0) * lanes
            spot = spot + lax.broadcasted_iota(jnp.int32, (per_circle, lanes), 1)
            for l in range(levels):
                piece = squared[c * per_circle : (c + 1) * per_circle, l * lanes : (l + 1) * lanes]
                piece = jnp.where(spot < n, piece, 0.0).astype(jnp.bfloat16)
                x_scr[start + c, 48 * l : 48 * l + per_circle, :] = piece


def circle_tables(g, chunk, wave, len_scr, table_scr, outer_scr):
    row = lax.broadcasted_iota(jnp.int32, (8, CHUNK), 0).astype(jnp.float32)
    wave_rows = row * wave
    length = len_scr[pl.ds(g, 1), :]
    inverse = 1.0 / length
    base = phase(wave_rows, length, inverse)
    outer = phase(wave_rows * float(FINE), length, inverse)
    outer_scr[chunk, g, 0:8, :] = outer[0]
    outer_scr[chunk, g, 8:16, :] = outer[1]
    step = times((base[0][7:8], base[1][7:8]), (base[0][1:2], base[1][1:2]))
    twice = jnp.broadcast_to(2.0 * step[0], base[0].shape)
    second = times(base, step)
    for part in range(2):
        rows = [base[part], second[part]]
        for q in range(2, FINE // 8):
            rows.append(twice * rows[-1] - rows[-2])
        table = jnp.concatenate(rows, axis=0).astype(jnp.bfloat16)
        table_scr[chunk, g, :, part * CHUNK : (part + 1) * CHUNK] = table


def transform_circle(g, chunk, levels, per_circle, x_scr, table_scr, outer_scr, coef_scr):
    outer = (outer_scr[chunk, g, 0:8, :], outer_scr[chunk, g, 8:16, :])
    jump = times((outer[0][7:8], outer[1][7:8]), (outer[0][1:2], outer[1][1:2]))
    jump = (jnp.broadcast_to(jump[0], (8, CHUNK)), jnp.broadcast_to(jump[1], (8, CHUNK)))
    x = x_scr[g]
    real = jnp.dot(x, table_scr[chunk, g, :, :CHUNK], preferred_element_type=jnp.float32)
    imag = jnp.dot(x, table_scr[chunk, g, :, CHUNK:], preferred_element_type=jnp.float32)
    for l in range(levels):
        last = per_circle // 8 - 1
        at = 48 * l + 8 * last
        total = (real[at : at + 8], imag[at : at + 8])
        for q in range(last - 1, -1, -1):
            at = 48 * l + 8 * q
            turned = times(total, jump)
            total = (turned[0] + real[at : at + 8], turned[1] + imag[at : at + 8])
        total = times(total, outer)
        for c in range(2):
            for block in range(CHUNK // 128):
                coef_scr[2 * l + c, block, 8 * g : 8 * g + 8, :] = total[c][:, block * 128 : (block + 1) * 128]


def pack_tiles(first, wave, top_wave, len_scr, coef_scr, send_scr):
    circles = len_scr.shape[0]
    quarter = lax.broadcasted_iota(jnp.int32, (circles, 128), 1) // 32
    for block in range(CHUNK // 128):
        cols = slice(block * 128, (block + 1) * 128)
        waves = wave[:, cols]
        live = (waves >= 1.0) & (waves < float(top_wave)) & (2.0 * waves < len_scr[:, cols])
        parts = []
        for k in range(4):
            rows = [coef_scr[k, block, pl.ds(r, circles, stride=8), :] for r in range(8)]
            while len(rows) > 1:
                rows = [rows[i] + rows[i + 1] for i in range(0, len(rows), 2)]
            parts.append(jnp.where(live, rows[0], 0.0))
        for to in range(4):
            value = parts[to]
            for k in range(4):
                if k != to:
                    value = jnp.where(quarter == k, pltpu.roll(parts[k], (32 * (k - to)) % 128, 1), value)
            send_scr[first + block * 4 + to] = value.astype(jnp.bfloat16)


def whole_kernel(
    top_wave, bands, groups, slot_dev,
    grid_ref, send_ref, donor_ref, tile_ref, kern_ref, len_hbm, wave_hbm, wave_rows_ref, legendre_ref, out_ref,
    pool_scr, diag_scr, send_scr, donor_scr, tile_scr, idx_scr, halo_scr, len_ref, slot_ref, wave_scr, waves_scr,
    x_scr, len_scr, table_scr, outer_scr, coef_scr, send_lat, recv_lat, send_lev, recv_lev, leg_scr,
    total_scr, sems, lat_sems, lev_sems, halo_sems, load_sems, leg_sems
):
    levels, blocks, lanes = grid_ref.shape
    cap = halo_scr.shape[1]
    circles = x_scr.shape[0]
    per_circle = blocks // circles
    band, group = lax.axis_index("lat"), lax.axis_index("lev")
    barrier = pltpu.get_barrier_semaphore()

    def greet_lat(i, carry):
        pl.semaphore_signal(barrier, inc=1, device_id={"lat": lax.rem(band + i, bands)}, device_id_type=MESH)
        return carry

    def greet_lev(i, carry):
        pl.semaphore_signal(barrier, inc=1, device_id={"lev": lax.rem(group + i, groups)}, device_id_type=MESH)
        return carry

    lax.fori_loop(1, bands, greet_lat, 0)
    lax.fori_loop(1, groups, greet_lev, 0)

    pairs = [(len_hbm, len_ref), (wave_rows_ref, wave_scr), (send_ref, send_scr), (donor_ref, donor_scr), (tile_ref, tile_scr)]
    for l in range(levels):
        cols = slice(l * lanes, (l + 1) * lanes)
        pairs.append((grid_ref.at[l], pool_scr.at[0:blocks, cols]))
    for l in range(levels):
        cols = slice(l * lanes, (l + 1) * lanes)
        pairs.append((kern_ref, diag_scr.at[:, cols, cols]))
    pairs.append((wave_hbm, slot_ref))
    loads = [pltpu.make_async_copy(src, dst, load_sems.at[i]) for i, (src, dst) in enumerate(pairs)]
    for load in loads:
        load.start()
    fetches = []
    for p in range(leg_scr.shape[0]):
        for k in range(slot_dev):
            rows = slice(p * leg_scr.shape[2], (p + 1) * leg_scr.shape[2])
            fetches.append(pltpu.make_async_copy(legendre_ref.at[k, rows], leg_scr.at[p, k], leg_sems.at[p, k]))
    for fetch in fetches:
        fetch.start()
    for l in range(levels):
        for m in range(levels):
            if l != m:
                rows, cols = slice(l * lanes, (l + 1) * lanes), slice(m * lanes, (m + 1) * lanes)
                diag_scr[:, rows, cols] = jnp.zeros((diag_scr.shape[0], lanes, lanes), jnp.bfloat16)
    idx_scr[...] = jnp.zeros_like(idx_scr)

    @pl.when(band == 0)
    def _():
        pool_scr[blocks : blocks + cap, :] = jnp.zeros((cap, levels * lanes), jnp.bfloat16)

    @pl.when(band == bands - 1)
    def _():
        pool_scr[blocks + cap : blocks + 2 * cap, :] = jnp.zeros((cap, levels * lanes), jnp.bfloat16)

    loads[0].wait()
    loads[1].wait()
    for g in range(circles):
        n = len_ref[band * circles + g]
        len_scr[g : g + 1, :] = jnp.full((1, CHUNK), n, jnp.int32).astype(jnp.float32)
    chunks = waves_scr.shape[0]
    each = CHUNK // 128
    for chunk in range(chunks):
        for k in range(each):
            at = chunk * each + k
            waves_scr[chunk, :, k * 128 : (k + 1) * 128] = wave_scr[at : at + 1, :].astype(jnp.float32)

    def table_step(step, carry):
        wave = waves_scr[step // (circles // PAIR)]
        for k in range(PAIR):
            g = step % (circles // PAIR) * PAIR + k
            circle_tables(g, step // (circles // PAIR), wave, len_scr, table_scr, outer_scr)
        return carry

    ahead = chunks * EARLY // 6 * (circles // PAIR)
    lax.fori_loop(0, ahead, table_step, 0)

    for load in loads[2:]:
        load.wait()
    idx_scr[0:2, :] = donor_scr[...].astype(jnp.float32)
    idx_scr[2:4, :] = tile_scr[...].astype(jnp.float32)
    idx_scr[4:6, 0:cap] = send_scr[0].astype(jnp.float32)
    columns = idx_scr[...].T
    own = lax.broadcasted_iota(jnp.int32, (cap, blocks), 1).astype(jnp.float32)
    for side in range(2):
        hot = jnp.where(own == columns[0:cap, 4 + side : 5 + side], 1.0, 0.0).astype(jnp.bfloat16)
        rows = jnp.dot(hot, pool_scr[0:blocks, :], preferred_element_type=jnp.float32)
        halo_scr[side] = rows.astype(jnp.bfloat16)
    pl.semaphore_wait(barrier, bands + groups - 2)

    down = pltpu.make_async_remote_copy(
        src_ref=halo_scr.at[0], dst_ref=pool_scr.at[blocks + cap : blocks + 2 * cap], send_sem=halo_sems.at[0],
        recv_sem=halo_sems.at[1], device_id={"lat": lax.rem(band + bands - 1, bands)}, device_id_type=MESH,
    )
    up = pltpu.make_async_remote_copy(
        src_ref=halo_scr.at[1], dst_ref=pool_scr.at[blocks : blocks + cap], send_sem=halo_sems.at[2],
        recv_sem=halo_sems.at[3], device_id={"lat": lax.rem(band + 1, bands)}, device_id_type=MESH,
    )

    @pl.when(band > 0)
    def _():
        down.start()

    @pl.when(band < bands - 1)
    def _():
        up.start()

    lax.fori_loop(ahead, chunks * (circles // PAIR), table_step, 0)

    @pl.when(band > 0)
    def _():
        down.wait_send()
        up.wait_recv()

    @pl.when(band < bands - 1)
    def _():
        up.wait_send()
        down.wait_recv()

    interpolate(band, len_ref, columns, pool_scr, diag_scr, x_scr)

    per_chunk = bands // chunks
    home = band // per_chunk

    def chunk_step(step, carry):
        chunk = lax.rem(step + 1 + home, chunks)
        wave = waves_scr[chunk]

        for g in range(circles):
            transform_circle(g, chunk, levels, per_circle, x_scr, table_scr, outer_scr, coef_scr)
        pack_tiles(chunk * per_chunk, wave, top_wave, len_scr, coef_scr, send_lat)
        for i in range(per_chunk):
            to = chunk * per_chunk + i

            @pl.when(to != band)
            def _():
                pltpu.make_async_remote_copy(
                    src_ref=send_lat.at[to], dst_ref=recv_lat.at[band], send_sem=sems.at[0],
                    recv_sem=lat_sems.at[home], device_id={"lat": to}, device_id_type=MESH,
                ).start()

        return carry

    lax.fori_loop(0, chunks, chunk_step, 0)
    recv_lat[band] = send_lat[band]
    next_band = {"lat": lax.rem(band + 1, bands)}
    next_group = {"lev": lax.rem(group + 1, groups)}

    def lat_wait(start, count, sem):
        some = pl.ds(start, count)
        return pltpu.make_async_remote_copy(
            src_ref=send_lat.at[some], dst_ref=recv_lat.at[some], send_sem=sems.at[0], recv_sem=sem,
            device_id=next_band, device_id_type=MESH,
        )

    def lev_wait(src, dst, sem):
        return pltpu.make_async_remote_copy(
            src_ref=src, dst_ref=dst, send_sem=sems.at[1], recv_sem=sem, device_id=next_group, device_id_type=MESH,
        )

    target = lax.broadcasted_iota(jnp.int32, (128, 128), 0)
    source = lax.broadcasted_iota(jnp.int32, (128, 128), 1)
    share = 4 * slot_dev
    wanted = (target % share) // slot_dev * (groups * slot_dev) + target // share * slot_dev + target % slot_dev
    pick = jnp.where(source == wanted, 1.0, 0.0).astype(jnp.bfloat16)
    span = per_chunk * circles
    for p in range(chunks):
        part = lax.rem(home + chunks - 1 - p, chunks)
        lat_wait(part * per_chunk, per_chunk - (p == chunks - 1), lat_sems.at[part]).wait_recv()
        arrived = recv_lat[pl.ds(part * per_chunk, per_chunk)].reshape(span, 128)
        turned = lax.dot_general(pick, arrived, (((1,), (1,)), ((), ())), preferred_element_type=jnp.float32)
        for v in range(groups):
            send_lev[p, v] = turned[v * share : (v + 1) * share].astype(jnp.bfloat16)

        def send_group(i, carry):
            to = lax.rem(group + i, groups)
            pltpu.make_async_remote_copy(
                src_ref=send_lev.at[p, to], dst_ref=recv_lev.at[p, group], send_sem=sems.at[1],
                recv_sem=lev_sems.at[p], device_id={"lev": to}, device_id_type=MESH,
            ).start()
            return carry

        lax.fori_loop(1, groups, send_group, 0)
        recv_lev[p, group] = send_lev[p, group]

    for fetch in fetches:
        fetch.wait()
    first = (band * groups + group) * slot_dev
    width = 256
    kinds = lax.broadcasted_iota(jnp.int32, (128, span), 0) % slot_dev
    for p in range(chunks):
        part = lax.rem(home + chunks - 1 - p, chunks)
        some = pl.ds(0, groups - 1)
        lev_wait(send_lev.at[p, some], recv_lev.at[p, some], lev_sems.at[p]).wait_recv()
        left = jnp.concatenate([recv_lev[p, v].astype(jnp.float32) for v in range(groups)], axis=0)
        left = jnp.concatenate([jnp.where(kinds == s, left, 0.0) for s in range(slot_dev)], axis=1).astype(jnp.bfloat16)
        for at in range(0, top_wave, width):
            cols = slice(at, at + width)
            right = leg_scr[part, :, :, cols].reshape(slot_dev * span, width)
            value = jnp.dot(left, right, preferred_element_type=jnp.float32)
            if p > 0:
                value = value + total_scr[:, cols]
            if p < chunks - 1:
                total_scr[:, cols] = value
                continue
            slot = lax.broadcasted_iota(jnp.int32, (128, width), 0) % slot_dev
            order = lax.broadcasted_iota(jnp.int32, (128, width), 1) + at
            least = jnp.zeros((128, width), jnp.int32)
            for s in range(slot_dev):
                least = jnp.where(slot == s, slot_ref[first + s], least)
            out_ref[:, cols] = jnp.where(order >= least, value, 0.0).astype(jnp.bfloat16)
    lat_wait(0, bands - 1, lat_sems.at[0]).wait_send()
    for p in range(chunks):
        some = pl.ds(0, groups - 1)
        lev_wait(send_lev.at[p, some], recv_lev.at[p, some], lev_sems.at[p]).wait_send()


def body(
    grid_field, send_blocks, donor_index, tile_choice, kernel_tiles, circle_len, slot_wave, legendre
):
    levels, blocks, lanes = grid_field.shape
    cap = send_blocks.shape[2]
    bands = lax.axis_size("lat")
    groups = lax.axis_size("lev")
    circles = blocks * lanes // PTS
    slots = slot_wave.shape[0]
    slot_dev, across, top_wave = legendre.shape
    share = 2 * levels * slot_dev
    tiles = kernel_tiles.shape[0]
    width = levels * lanes
    chunks = slots // CHUNK
    bf16, f32, i32 = jnp.bfloat16, jnp.float32, jnp.int32
    hbm = pl.BlockSpec(memory_space=pltpu.HBM)
    spectra = pl.pallas_call(
        functools.partial(whole_kernel, top_wave, bands, groups, slot_dev),
        out_shape=jax.ShapeDtypeStruct((groups * share, top_wave), bf16),
        in_specs=[hbm] * 9,
        out_specs=pl.BlockSpec(memory_space=pltpu.VMEM),
        scratch_shapes=[
            pltpu.VMEM((blocks + 2 * cap, width), bf16),
            pltpu.VMEM((tiles, width, width), bf16),
            pltpu.VMEM((1, 2, cap), i32),
            pltpu.VMEM((2, blocks), i32),
            pltpu.VMEM((2, blocks), i32),
            pltpu.VMEM((8, blocks), f32),
            pltpu.VMEM((2, cap, width), bf16),
            pltpu.SMEM(circle_len.shape, i32),
            pltpu.SMEM(slot_wave.shape, i32),
            pltpu.VMEM((slots // 128, 128), i32),
            pltpu.VMEM((chunks, 1, CHUNK), f32),
            pltpu.VMEM((circles, 96, lanes), bf16),
            pltpu.VMEM((circles, CHUNK), f32),
            pltpu.VMEM((chunks, circles, FINE, 2 * CHUNK), bf16),
            pltpu.VMEM((chunks, circles, 16, CHUNK), f32),
            pltpu.VMEM((2 * levels, CHUNK // 128, 8 * circles, 128), f32),
            pltpu.VMEM((bands, circles, 128), bf16),
            pltpu.VMEM((bands, circles, 128), bf16),
            pltpu.VMEM((chunks, groups, share, across // chunks), bf16),
            pltpu.VMEM((chunks, groups, share, across // chunks), bf16),
            pltpu.VMEM((chunks, slot_dev, across // chunks, top_wave), bf16),
            pltpu.VMEM((groups * share, top_wave), f32),
            pltpu.SemaphoreType.DMA((2,)),
            pltpu.SemaphoreType.DMA((chunks,)),
            pltpu.SemaphoreType.DMA((chunks,)),
            pltpu.SemaphoreType.DMA((4,)),
            pltpu.SemaphoreType.DMA((10,)),
            pltpu.SemaphoreType.DMA((chunks, slot_dev)),
        ],
        compiler_params=pltpu.CompilerParams(
            vmem_limit_bytes=40 * 1024 * 1024, collective_id=0, has_side_effects=True
        ),
        name="interpolate_transform_exchange",
    )(
        *(
            pltpu.with_memory_space_constraint(array, pltpu.HBM)
            for array in (
                grid_field, send_blocks, donor_index.T, tile_choice.T, kernel_tiles, circle_len, slot_wave,
                slot_wave.reshape(slots // 128, 128), legendre,
            )
        )
    )
    return spectra.reshape(groups * levels, 2, slot_dev, top_wave)


def solution(mesh):
    return jax.shard_map(
        body,
        mesh=mesh,
        in_specs=(
            P("lev", "lat", None),
            P("lat", None, None),
            P("lat", None),
            P("lat", None),
            P(),
            P(),
            P(),
            P(("lat", "lev"), None, None),
        ),
        out_specs=P(None, None, ("lat", "lev"), None),
        check_vma=False,
    )
```
